32 devices in a mesh: dp: 4 (over y, x), seq: 4 (over z), head: 2 (over core).
Axes of the slice: x: 2, y: 2, z: 4, core: 2. Of those that a mesh axis runs over, the one named last changes fastest.
Arguments:
- latents: bfloat16 [4, 1024, 2048], P('dp', 'seq'), may hold values from -6 to 6
- w_qkv: bfloat16 [2048, 3, 1536], P(None, None, 'head'), may hold values from -0.125 to 0.125
- q_gain: float32 [128], replicated, may hold values from 0.1 to 1.9
- k_gain: float32 [128], replicated, may hold values from 0.1 to 1.9
- neighbours: int32 [16, 9], replicated, may hold values from -1 to 15, as said below
- grad_out: bfloat16 [4, 1024, 1536], P('dp', 'seq', 'head'), may hold values from -6 to 6
Outputs:
- attn_out: bfloat16 [4, 1024, 1536], P('dp', 'seq', 'head')
- grad_x: bfloat16 [4, 1024, 2048], P('dp', ('seq', 'head'))
- grad_w: float32 [2048, 3, 1536], P(('dp', 'seq'), None, 'head')
The draws below stay inside these ranges and needn't reach their ends.
Inputs may be any that keep to these rules, and one draw needn't show every extreme that they name: `neighbours`: row t lists only tiles whose slab differs from that of t (t // 4) by at most one and whose position in the slab (index % 4) differs by at most one, each at most once; t itself is always listed.
All inputs are finite; a program needn't handle non-finite values.
Results may differ from the reference program's by a relative error of at most 0.017.
Values may be sent and summed in bfloat16 or wider, within the bound.
A program may use at most 128 MiB of HBM per device.

```python
import math
import jax
import jax.numpy as jnp
from jax import lax

D = 2048
HEADS = 12
HD = 128
TILE = 64
GS = 4
SLAB = 256
TILES = 16
TOKENS = 1024
CLIPS = 4
HH = 1536


def draw_neighbours(key, part):
    tile_ids = jnp.arange(TILES, dtype=jnp.int32)
    slab_ids = tile_ids // GS
    column = tile_ids % GS
    reach = jax.random.randint(key, (TILES, 2), 0, 4)
    time_open = reach[:, 0] > 0
    space_open = reach[:, 1] > 0
    entries = []
    for time_step in (-1, 0, 1):
        for space_step in (-1, 0, 1):
            other_slab = slab_ids + time_step
            other_column = column + space_step
            inside = (other_slab >= 0) & (other_slab < TILES // GS) & (other_column >= 0) & (other_column < GS)
            open_time = jnp.logical_or(time_step == 0, time_open)
            open_space = jnp.logical_or(space_step == 0, space_open)
            keep = inside & open_time & open_space
            entries.append(jnp.where(keep, other_slab * GS + other_column, -1))
    return jnp.stack(entries, axis=1).astype(jnp.int32)


def with_spikes(values, own_key, source, target, shards_of, factor):
    def block_of(dim):
        return (jnp.arange(values.shape[dim]) // (values.shape[dim] // shards_of)).reshape((-1,) + (1,) * (values.ndim - 1 - dim))

    near = jax.random.permutation(own_key, shards_of)[block_of(target)]
    second = (block_of(target) + shards_of // 2) % shards_of
    return jnp.where((block_of(source) == near) | (block_of(source) == second), factor * values, values)


def block_scale(stream_key, dims, split, low, largest):
    level = 1.0
    for position, blocks in split:
        draws = jax.random.uniform(jax.random.fold_in(jax.random.fold_in(stream_key, 6), position), (blocks,), jnp.float32, low / len(split), largest / len(split))
        level = level * jnp.repeat(jnp.exp(draws), dims[position] // blocks).reshape((-1,) + (1,) * (len(dims) - 1 - position))
    return level


def normal_values(key, dims, deviation, most, shards=(), kind=jnp.bfloat16):
    array = jax.random.normal(key, dims, jnp.float32) * deviation
    if len(shards) > 0:
        array = block_scale(key, dims, shards, -0.22, 0.18) * array
    return jnp.clip(array, min=-most, max=most).astype(kind)


def gaussian_with(own_key, shape, deviation, most, pieces, heavy, held_as=jnp.bfloat16):
    array = deviation * jax.random.normal(own_key, shape, jnp.float32)
    if pieces:
        array = array * block_scale(own_key, shape, pieces, -0.22, 0.18)
    return jnp.clip(with_spikes(array, jax.random.fold_in(own_key, 3), *heavy), -most, most).astype(held_as)


def setup_inputs(seed: int = 0) -> dict:
    splits = jax.random.split(jax.random.key(seed), 7)
    return {
        "latents": gaussian_with(splits[0], (CLIPS, TOKENS, D), 1.0, 6.0, ((0, 4), (1, 4)), (1, 2, 4, 2.0)),
        "w_qkv": normal_values(splits[1], (D, 3, HH), D ** -0.5, 0.125, ((2, 2),)),
        "q_gain": jnp.clip(1.0 + 0.18 * jax.random.normal(splits[2], (HD,), jnp.float32), 0.1, 1.9),
        "k_gain": jnp.clip(1.0 + 0.18 * jax.random.normal(splits[3], (HD,), jnp.float32), 0.1, 1.9),
        "neighbours": draw_neighbours(jax.random.fold_in(splits[6], 71), 0),
        "grad_out": normal_values(splits[5], (CLIPS, TOKENS, HH), 1.0, 6.0, ((0, 4), (1, 4), (2, 2))),
    }


EPS = 1e-06

def inv_rms(values):
    return lax.rsqrt(lax.optimization_barrier(jnp.mean(values * values, axis=-1, keepdims=True)) + EPS)

def norm_back(raw, inverse, gain, upstream):
    normed = raw * inverse
    weighted = upstream * gain
    return inverse * (weighted - normed * lax.optimization_barrier(jnp.mean(weighted * normed, axis=-1, keepdims=True)))

def slab_allowed(neighbours, slab_index, tiles_slab):
    tile_total = neighbours.shape[0]
    first_query = (slab_index * tiles_slab).astype(jnp.int32)
    picked = lax.dynamic_slice_in_dim(neighbours, first_query, tiles_slab, 0)
    key_ids = (slab_index - 1) * tiles_slab + jnp.arange(3 * tiles_slab, dtype=jnp.int32)
    valid = (key_ids >= 0) & (key_ids < tile_total)
    hits = jnp.any(picked[:, :, None] == key_ids[None, None, :], axis=1) & valid[None, :]
    block = jnp.where(hits, 1.0, 0.0).astype(jnp.float32)
    return jnp.repeat(jnp.repeat(block, TILE, axis=0), TILE, axis=1)

def fold_rims(parts):
    lower = parts[:, :SLAB]
    middle = parts[:, SLAB:2 * SLAB]
    upper = parts[:, 2 * SLAB:]
    from_below = jnp.concatenate([jnp.zeros_like(upper[:1]), upper[:-1]], axis=0)
    from_above = jnp.concatenate([lower[1:], jnp.zeros_like(lower[:1])], axis=0)
    summed = middle + from_below + from_above
    return summed.reshape(summed.shape[0] * SLAB, HEADS, HD)

def clip_pass(latent_clip, cot_clip, w_flat, q_gain, k_gain, neighbours):
    token_count = latent_clip.shape[0]
    slab_count = token_count // SLAB
    score_scale = 1.0 / math.sqrt(HD)
    qkv = jnp.dot(latent_clip, w_flat, preferred_element_type=jnp.float32).reshape(token_count, 3, HEADS, HD)
    q_raw = qkv[:, 0]
    k_raw = qkv[:, 1]
    v_raw = qkv[:, 2]
    q_inv = inv_rms(q_raw)
    k_inv = inv_rms(k_raw)
    q_hat = lax.optimization_barrier((q_raw * q_inv * q_gain).astype(jnp.bfloat16))
    k_hat = lax.optimization_barrier((k_raw * k_inv * k_gain).astype(jnp.bfloat16))
    v_hat = lax.optimization_barrier(v_raw.astype(jnp.bfloat16))
    pad_keys = jnp.pad(k_hat, ((SLAB, SLAB), (0, 0), (0, 0)))
    pad_values = jnp.pad(v_hat, ((SLAB, SLAB), (0, 0), (0, 0)))

    def one_slab(slab_index):
        offset = (slab_index * SLAB).astype(jnp.int32)
        queries = lax.dynamic_slice_in_dim(q_hat, offset, SLAB, 0).astype(jnp.float32)
        keys = lax.dynamic_slice_in_dim(pad_keys, offset, 3 * SLAB, 0).astype(jnp.float32)
        values = lax.dynamic_slice_in_dim(pad_values, offset, 3 * SLAB, 0).astype(jnp.float32)
        upstream = lax.dynamic_slice_in_dim(cot_clip, offset, SLAB, 0).astype(jnp.float32)
        upstream = upstream.reshape(SLAB, HEADS, HD)
        allowed = slab_allowed(neighbours, slab_index, GS)
        scores = jnp.einsum('qhe,khe->hqk', queries, keys) * score_scale
        exponent = jnp.exp(scores) * allowed[None]
        row_total = lax.optimization_barrier(jnp.sum(exponent, axis=-1, keepdims=True))
        probs = exponent / row_total
        probs_b = lax.optimization_barrier(probs.astype(jnp.bfloat16)).astype(jnp.float32)
        attended = jnp.einsum('hqk,khe->qhe', probs_b, values)
        d_probs = jnp.einsum('qhe,khe->hqk', upstream, values)
        row_delta = lax.optimization_barrier(jnp.sum(probs * d_probs, axis=-1, keepdims=True))
        d_scores = (probs * (d_probs - row_delta) * score_scale).astype(jnp.bfloat16)
        d_scores = lax.optimization_barrier(d_scores).astype(jnp.float32)
        d_query = jnp.einsum('hqk,khe->qhe', d_scores, keys)
        d_keys = jnp.einsum('hqk,qhe->khe', d_scores, queries)
        d_values = jnp.einsum('hqk,qhe->khe', probs_b, upstream)
        return (attended.astype(jnp.bfloat16), d_query, d_keys, d_values)
    attended, d_qhat, d_kparts, d_vparts = lax.map(one_slab, jnp.arange(slab_count, dtype=jnp.int32))
    attended = attended.reshape(token_count, HEADS * HD)
    d_qhat = d_qhat.reshape(token_count, HEADS, HD)
    d_khat = fold_rims(d_kparts)
    d_value = fold_rims(d_vparts)
    d_query = norm_back(q_raw, q_inv, q_gain, d_qhat)
    d_key = norm_back(k_raw, k_inv, k_gain, d_khat)
    d_qkv = jnp.stack([d_query, d_key, d_value], axis=1).astype(jnp.bfloat16).reshape(token_count, 3 * HEADS * HD)
    grad_latent = jnp.dot(d_qkv, w_flat.T, preferred_element_type=jnp.float32).astype(jnp.bfloat16)
    weight_part = jnp.dot(latent_clip.T, d_qkv, preferred_element_type=jnp.float32)
    return (attended, grad_latent, weight_part)

def reference(latents, w_qkv, q_gain, k_gain, neighbours, grad_out):
    w_flat = w_qkv.reshape(D, 3 * HEADS * HD)

    def per_clip(pair):
        return clip_pass(pair[0], pair[1], w_flat, q_gain, k_gain, neighbours)
    attn_out, grad_x, weight_parts = lax.map(per_clip, (latents, grad_out))
    grad_w = lax.optimization_barrier(jnp.sum(weight_parts, axis=0)).reshape(D, 3, HEADS * HD)
    return (attn_out, grad_x, grad_w)
```

```python
import functools
import math

import jax
import jax.numpy as jnp
from jax import lax
from jax.experimental import pallas as pl
from jax.experimental.pallas import tpu as pltpu
from jax.sharding import PartitionSpec as P

MESH = pl.DeviceIdType.MESH

HD = 128
TILE = 64


EPS = 1e-06


def with_halo(block, sides, width):
    for axis, dim in sides:
        count = lax.axis_size(axis)
        forward = [(i, i + 1) for i in range(count - 1)]
        backward = [(target, source) for source, target in forward]
        low = lax.ppermute(
            lax.slice_in_dim(block, block.shape[dim] - width, None, axis=dim), axis, forward
        )
        high = lax.ppermute(lax.slice_in_dim(block, 0, width, axis=dim), axis, backward)
        block = jnp.concatenate([low, block, high], axis=dim)
    return block


def inv_rms(values):
    return lax.rsqrt(jnp.mean(values * values, axis=-1, keepdims=True) + EPS)


def norm_back(raw, inverse, gain, upstream):
    normed = raw * inverse
    weighted = upstream * gain
    return inverse * (weighted - normed * jnp.mean(weighted * normed, axis=-1, keepdims=True))


def tile_allowed(neighbours, query_first, query_count, key_first, key_count):
    tile_total = neighbours.shape[0]
    padded = jnp.pad(neighbours, ((query_count, query_count), (0, 0)), constant_values=-1)
    picked = lax.dynamic_slice_in_dim(padded, query_first + query_count, query_count, 0)
    query_ids = query_first + jnp.arange(query_count, dtype=jnp.int32)
    key_ids = key_first + jnp.arange(key_count, dtype=jnp.int32)
    query_valid = (query_ids >= 0) & (query_ids < tile_total)
    key_valid = (key_ids >= 0) & (key_ids < tile_total)
    hits = jnp.any(picked[:, :, None] == key_ids[None, None, :], axis=1)
    hits = hits & query_valid[:, None] & key_valid[None, :]
    block = jnp.where(hits, 1.0, 0.0).astype(jnp.float32)
    return jnp.repeat(jnp.repeat(block, TILE, axis=0), TILE, axis=1)


def remote(src, dst, send_sem, recv_sem, peer):
    return pltpu.make_async_remote_copy(
        src_ref=src,
        dst_ref=dst,
        send_sem=send_sem,
        recv_sem=recv_sem,
        device_id=peer,
        device_id_type=MESH,
    )


def grads_kernel(
    n_dp, n_seq, n_head, dq_ref, lat_ref, w_ref, gw_ref, gx_ref,
    gath, w_buf, part, z_send, z_recv, gx_acc, gx_recv,
    w_sem, d_ss, d_rs, z_ss, z_rs, h_ss, h_rs,
):
    chunks, slab, width = dq_ref.shape
    rows = part.shape[1]
    half = gx_ref.shape[0]
    me_dp = lax.axis_index("dp")
    me_seq = lax.axis_index("seq")
    me_head = lax.axis_index("head")
    relay = n_dp == 4

    def dp_peer(step):
        if relay:
            low, high = lax.rem(me_dp, 2), me_dp // 2
            if step % 2:
                low = 1 - low
            if step // 2:
                high = 1 - high
            return {"dp": high * 2 + low}
        return {"dp": lax.rem(me_dp + step, n_dp)}

    def dp_source(step):
        if relay:
            return dp_peer(step)
        return {"dp": lax.rem(me_dp + n_dp - step, n_dp)}

    direct = (1, 2) if relay else tuple(range(1, n_dp))

    def seq_peer(step):
        return lax.rem(me_seq + step, n_seq)

    def head_peer(step):
        return lax.rem(me_head + step, n_head)

    def w_copy(c):
        return pltpu.make_async_copy(
            w_ref.at[:, pl.ds(pl.multiple_of(c * width, width), width)],
            w_buf.at[c],
            w_sem.at[c],
        )

    @pl.loop(0, chunks)
    def _(c):
        w_copy(c).start()

    barrier = pltpu.get_barrier_semaphore()
    greeted = 0
    for step in direct:
        pl.semaphore_signal(barrier, inc=1, device_id=dp_source(step), device_id_type=MESH)
        greeted += 1
    for step in range(1, n_seq):
        pl.semaphore_signal(
            barrier, inc=1, device_id={"seq": seq_peer(step)}, device_id_type=MESH
        )
        greeted += 1
    for step in range(1, n_head):
        pl.semaphore_signal(
            barrier, inc=1, device_id={"head": head_peer(step)}, device_id_type=MESH
        )
        greeted += 1
    pl.semaphore_wait(barrier, greeted)

    def dp_copy(c, step):
        return remote(
            dq_ref.at[c], gath.at[c, step - 1],
            d_ss.at[c, step - 1], d_rs.at[c, step - 1], dp_peer(step),
        )

    def relay_copy(c, via, onward):
        return remote(
            gath.at[c, via - 1], gath.at[c, 2], d_ss.at[c, 2], d_rs.at[c, 2], dp_peer(onward)
        )

    @pl.loop(0, chunks)
    def _(c):
        for step in direct:
            dp_copy(c, step).start()

    gx_acc[...] = jnp.zeros_like(gx_acc)

    def z_copy(c, step):
        return remote(
            z_send.at[c, seq_peer(step)], z_recv.at[c, step - 1],
            z_ss.at[c, step - 1], z_rs.at[c, step - 1], {"seq": seq_peer(step)},
        )

    def input_share(c):
        w_copy(c).wait()
        gx_acc[...] += lax.dot_general(
            dq_ref[c], w_buf[c], (((1,), (1,)), ((), ())), preferred_element_type=jnp.float32
        )

    def weight_share(c):
        if relay:
            relay_copy(c, 1, 2).wait_recv()
        others = gath[c].reshape((n_dp - 1) * slab, width)
        product = jnp.dot(lat_ref[:, :slab], dq_ref[c], preferred_element_type=jnp.float32)
        product += jnp.dot(lat_ref[:, slab:], others, preferred_element_type=jnp.float32)
        product = product.reshape(n_seq, rows, width)
        part[...] = product
        z_send[c] = product.astype(jnp.bfloat16)
        for step in range(n_seq - 1, 0, -1):
            z_copy(c, step).start()
        gw_ref[c] = part[me_seq]

    @pl.loop(0, chunks)
    def _(c):
        for step in direct:
            dp_copy(c, step).wait_recv()
        if relay:
            @pl.when(lax.rem(c, 2) == 0)
            def _():
                relay_copy(c, 1, 2).start()

            @pl.when(lax.rem(c, 2) == 1)
            def _():
                relay_copy(c, 2, 1).start()

        input_share(c)

        @pl.when(c > 0)
        def _():
            weight_share(c - 1)

    def h_copy(step):
        return remote(
            gx_acc.at[pl.ds(pl.multiple_of(head_peer(step) * half, half), half)],
            gx_recv.at[step - 1], h_ss.at[step - 1], h_rs.at[step - 1],
            {"head": head_peer(step)},
        )

    for step in range(1, n_head):
        h_copy(step).start()
    weight_share(chunks - 1)
    for step in range(1, n_head):
        h_copy(step).wait()
    total = gx_acc[pl.ds(pl.multiple_of(me_head * half, half), half)]
    for step in range(1, n_head):
        total = total + gx_recv[step - 1]
    gx_ref[...] = total.astype(gx_ref.dtype)

    @pl.loop(0, chunks)
    def _(c):
        for step in range(1, n_seq):
            z_copy(c, step).wait()
        share = gw_ref[c]
        for step in range(1, n_seq):
            share = share + z_recv[c, step - 1].astype(jnp.float32)
        gw_ref[c] = share
        for step in direct:
            dp_copy(c, step).wait_send()
        if relay:
            relay_copy(c, 1, 2).wait_send()


def grads(d_chunks, lat_t, flat_w):
    n_dp, n_seq, n_head = (lax.axis_size(axis) for axis in ("dp", "seq", "head"))
    chunks, slab, width = d_chunks.shape
    model_width = flat_w.shape[0]
    rows = model_width // (n_dp * n_seq)
    half = slab // n_head
    vmem = pl.BlockSpec(memory_space=pltpu.VMEM)
    dma = pltpu.SemaphoreType.DMA
    return pl.pallas_call(
        functools.partial(grads_kernel, n_dp, n_seq, n_head),
        out_shape=(
            jax.ShapeDtypeStruct((chunks, rows, width), jnp.float32),
            jax.ShapeDtypeStruct((half, model_width), jnp.bfloat16),
        ),
        in_specs=[vmem, vmem, pl.BlockSpec(memory_space=pl.ANY)],
        out_specs=(vmem, vmem),
        scratch_shapes=[
            pltpu.VMEM((chunks, n_dp - 1, slab, width), jnp.bfloat16),
            pltpu.VMEM((chunks, model_width, width), jnp.bfloat16),
            pltpu.VMEM((n_seq, rows, width), jnp.float32),
            pltpu.VMEM((chunks, n_seq, rows, width), jnp.bfloat16),
            pltpu.VMEM((chunks, n_seq - 1, rows, width), jnp.bfloat16),
            pltpu.VMEM((slab, model_width), jnp.float32),
            pltpu.VMEM((n_head - 1, half, model_width), jnp.float32),
            dma((chunks,)),
            dma((chunks, n_dp - 1)),
            dma((chunks, n_dp - 1)),
            dma((chunks, n_seq - 1)),
            dma((chunks, n_seq - 1)),
            dma((n_head - 1,)),
            dma((n_head - 1,)),
        ],
        compiler_params=pltpu.CompilerParams(
            collective_id=0, has_side_effects=True, vmem_limit_bytes=60 * 1024 * 1024
        ),
        name="grads",
    )(d_chunks, lat_t, flat_w)


def clip_columns(slab_tokens):
    n_dp = lax.axis_size("dp")
    me = lax.axis_index("dp")
    width = slab_tokens.shape[1] // n_dp
    pieces = []
    for step in range(n_dp):
        if n_dp == 4:
            pairs = [(i, i ^ step) for i in range(n_dp)]
            target = me ^ step
        else:
            pairs = [(i, (i + step) % n_dp) for i in range(n_dp)]
            target = lax.rem(me + step, n_dp)
        piece = lax.dynamic_slice_in_dim(slab_tokens, target * width, width, 1)
        pieces.append(lax.ppermute(piece, "dp", pairs) if step else piece)
    return jnp.transpose(jnp.concatenate(pieces, axis=0))


def local(latents, w_qkv, q_gain, k_gain, neighbours, grad_out):
    slab_tokens = latents[0]
    slab_rows = slab_tokens.shape[0]
    model_width = w_qkv.shape[0]
    head_width = w_qkv.shape[2]
    head_count = head_width // HD
    tiles_slab = slab_rows // TILE
    score_scale = 1.0 / math.sqrt(HD)
    flat_w = w_qkv.reshape(model_width, 3 * head_width)
    qkv = jnp.dot(slab_tokens, flat_w, preferred_element_type=jnp.float32).reshape(
        slab_rows, 3, head_count, HD
    )
    q_raw = qkv[:, 0]
    k_raw = qkv[:, 1]
    v_raw = qkv[:, 2]
    q_inv = inv_rms(q_raw)
    k_inv = inv_rms(k_raw)
    q_hat = (q_raw * q_inv * q_gain).astype(jnp.bfloat16)
    k_hat = (k_raw * k_inv * k_gain).astype(jnp.bfloat16)
    v_hat = v_raw.astype(jnp.bfloat16)
    stacked = jnp.stack(
        [k_hat.reshape(slab_rows, head_width), v_hat.reshape(slab_rows, head_width)], axis=1
    )
    widened = with_halo(stacked, (("seq", 0),), slab_rows)
    keys_wide = widened[:, 0].reshape(3 * slab_rows, head_count, HD)
    values_wide = widened[:, 1].reshape(3 * slab_rows, head_count, HD)
    seq_slab = lax.axis_index("seq")
    own_tile = seq_slab * tiles_slab
    first_tile = (seq_slab - 1) * tiles_slab
    allowed = tile_allowed(neighbours, own_tile, tiles_slab, first_tile, 3 * tiles_slab)
    scores = (
        jnp.einsum("qhe,khe->hqk", q_hat, keys_wide, preferred_element_type=jnp.float32)
        * score_scale
    )
    exponent = jnp.exp(scores) * allowed[None]
    row_total = jnp.sum(exponent, axis=-1)
    probs = exponent / row_total[..., None]
    probs_b = probs.astype(jnp.bfloat16)
    attended = jnp.einsum("hqk,khe->qhe", probs_b, values_wide, preferred_element_type=jnp.float32)
    attn_out = attended.astype(jnp.bfloat16).reshape(1, slab_rows, head_width)
    upstream = grad_out[0].reshape(slab_rows, head_count, HD)
    d_probs = jnp.einsum("qhe,khe->hqk", upstream, values_wide, preferred_element_type=jnp.float32)
    row_delta = jnp.sum(probs * d_probs, axis=-1)
    d_scores = (probs * (d_probs - row_delta[..., None]) * score_scale).astype(jnp.bfloat16)
    d_qhat = jnp.einsum("hqk,khe->qhe", d_scores, keys_wide, preferred_element_type=jnp.float32)
    query_pack = jnp.stack([q_hat.reshape(slab_rows, head_width), grad_out[0]], axis=1)
    row_stats = jnp.transpose(jnp.stack([row_total, row_delta], axis=0), (2, 0, 1))
    pack_wide = with_halo(query_pack, (("seq", 0),), slab_rows)
    stats_wide = with_halo(row_stats, (("seq", 0),), slab_rows)
    queries_wide = pack_wide[:, 0].reshape(3 * slab_rows, head_count, HD)
    upstream_wide = pack_wide[:, 1].reshape(3 * slab_rows, head_count, HD)
    total_wide = jnp.transpose(stats_wide[:, 0])
    delta_wide = jnp.transpose(stats_wide[:, 1])
    safe_total = jnp.where(total_wide > 0.0, total_wide, 1.0)
    reverse_allowed = tile_allowed(neighbours, first_tile, 3 * tiles_slab, own_tile, tiles_slab)
    scores_back = (
        jnp.einsum("qhe,khe->hqk", queries_wide, k_hat, preferred_element_type=jnp.float32)
        * score_scale
    )
    probs_back = jnp.exp(scores_back) * reverse_allowed[None] / safe_total[..., None]
    probs_back_b = probs_back.astype(jnp.bfloat16)
    d_probs_back = jnp.einsum(
        "qhe,khe->hqk", upstream_wide, v_hat, preferred_element_type=jnp.float32
    )
    d_scores_back = (probs_back * (d_probs_back - delta_wide[..., None]) * score_scale).astype(
        jnp.bfloat16
    )
    d_khat = jnp.einsum(
        "hqk,qhe->khe", d_scores_back, queries_wide, preferred_element_type=jnp.float32
    )
    d_value = jnp.einsum(
        "hqk,qhe->khe", probs_back_b, upstream_wide, preferred_element_type=jnp.float32
    )
    d_query = norm_back(q_raw, q_inv, q_gain, d_qhat)
    d_key = norm_back(k_raw, k_inv, k_gain, d_khat)
    d_qkv = (
        jnp.stack([d_query, d_key, d_value], axis=1)
        .astype(jnp.bfloat16)
        .reshape(slab_rows, 3 * head_width)
    )
    width = 3 * HD
    chunks = 3 * head_width // width
    d_chunks = jnp.transpose(d_qkv.reshape(slab_rows, chunks, width), (1, 0, 2))
    share, grad_rows = grads(d_chunks, clip_columns(slab_tokens), flat_w)
    grad_x = grad_rows[None]
    grad_w = jnp.transpose(share, (1, 0, 2)).reshape(share.shape[1], 3, head_width)
    return (attn_out, grad_x, grad_w)


def solution(mesh):
    in_specs = (P("dp", "seq", None), P(None, None, "head"), P(), P(), P(), P("dp", "seq", "head"))
    out_specs = (
        P("dp", "seq", "head"),
        P("dp", ("seq", "head"), None),
        P(("dp", "seq"), None, "head"),
    )
    return jax.shard_map(local, mesh=mesh, in_specs=in_specs, out_specs=out_specs, check_vma=False)
```

```python
import functools
import math

import jax
import jax.numpy as jnp
from jax import lax
from jax.experimental import pallas as pl
from jax.experimental.pallas import tpu as pltpu
from jax.sharding import PartitionSpec as P

MESH = pl.DeviceIdType.MESH

HD = 128
TILE = 64


EPS = 1e-06


def inv_rms(values):
    return lax.rsqrt(jnp.mean(values * values, axis=-1, keepdims=True) + EPS)


def norm_back(raw, inverse, gain, upstream):
    normed = raw * inverse
    weighted = upstream * gain
    return inverse * (weighted - normed * jnp.mean(weighted * normed, axis=-1, keepdims=True))


def remote(src, dst, send_sem, recv_sem, peer):
    return pltpu.make_async_remote_copy(
        src_ref=src,
        dst_ref=dst,
        send_sem=send_sem,
        recv_sem=recv_sem,
        device_id=peer,
        device_id_type=MESH,
    )


def grads_kernel(
    n_dp, n_seq, n_head, dq_ref, lat_ref, w_ref, gw_ref, gx_ref,
    gath, w_buf, part, z_send, z_recv, gx_acc, gx_recv,
    w_sem, d_ss, d_rs, z_ss, z_rs, h_ss, h_rs,
):
    chunks, slab, width = dq_ref.shape
    rows = part.shape[1]
    half = gx_ref.shape[0]
    me_dp = lax.axis_index("dp")
    me_seq = lax.axis_index("seq")
    me_head = lax.axis_index("head")
    relay = n_dp == 4
    parts = chunks // w_ref.shape[0]

    def cols(c):
        return pl.ds(pl.multiple_of(lax.rem(c, parts) * width, width), width)

    def dp_peer(step):
        if relay:
            low, high = lax.rem(me_dp, 2), me_dp // 2
            if step % 2:
                low = 1 - low
            if step // 2:
                high = 1 - high
            return {"dp": high * 2 + low}
        return {"dp": lax.rem(me_dp + step, n_dp)}

    def dp_source(step):
        if relay:
            return dp_peer(step)
        return {"dp": lax.rem(me_dp + n_dp - step, n_dp)}

    direct = (1, 2) if relay else tuple(range(1, n_dp))

    def seq_peer(step):
        return lax.rem(me_seq + step, n_seq)

    def head_peer(step):
        return lax.rem(me_head + step, n_head)

    def w_copy(c):
        return pltpu.make_async_copy(w_ref.at[c // parts, :, cols(c)], w_buf.at[c], w_sem.at[c])

    @pl.loop(0, chunks)
    def _(c):
        w_copy(c).start()

    barrier = pltpu.get_barrier_semaphore()
    greeted = 0
    for step in direct:
        pl.semaphore_signal(barrier, inc=1, device_id=dp_source(step), device_id_type=MESH)
        greeted += 1
    for step in range(1, n_seq):
        pl.semaphore_signal(
            barrier, inc=1, device_id={"seq": seq_peer(step)}, device_id_type=MESH
        )
        greeted += 1
    for step in range(1, n_head):
        pl.semaphore_signal(
            barrier, inc=1, device_id={"head": head_peer(step)}, device_id_type=MESH
        )
        greeted += 1
    pl.semaphore_wait(barrier, greeted)

    def dp_copy(c, step):
        return remote(
            dq_ref.at[c], gath.at[c, step - 1],
            d_ss.at[c, step - 1], d_rs.at[c, step - 1], dp_peer(step),
        )

    def relay_copy(c, via, onward):
        return remote(
            gath.at[c, via - 1], gath.at[c, 2], d_ss.at[c, 2], d_rs.at[c, 2], dp_peer(onward)
        )

    @pl.loop(0, chunks)
    def _(c):
        for step in direct:
            dp_copy(c, step).start()

    gx_acc[...] = jnp.zeros_like(gx_acc)

    def z_copy(c, step):
        return remote(
            z_send.at[c, seq_peer(step)], z_recv.at[c, step - 1],
            z_ss.at[c, step - 1], z_rs.at[c, step - 1], {"seq": seq_peer(step)},
        )

    def input_share(c):
        w_copy(c).wait()
        gx_acc[...] += lax.dot_general(
            dq_ref[c], w_buf[c], (((1,), (1,)), ((), ())), preferred_element_type=jnp.float32
        )

    def weight_share(c):
        if relay:
            relay_copy(c, 1, 2).wait_recv()
        others = gath[c].reshape((n_dp - 1) * slab, width)
        product = jnp.dot(lat_ref[:, :slab], dq_ref[c], preferred_element_type=jnp.float32)
        product += jnp.dot(lat_ref[:, slab:], others, preferred_element_type=jnp.float32)
        product = product.reshape(n_seq, rows, width)
        part[...] = product
        z_send[c] = product.astype(jnp.bfloat16)
        for step in range(n_seq - 1, 0, -1):
            z_copy(c, step).start()
        gw_ref[c // parts, :, cols(c)] = part[me_seq]

    @pl.loop(0, chunks)
    def _(c):
        for step in direct:
            dp_copy(c, step).wait_recv()
        if relay:
            @pl.when(lax.rem(c, 2) == 0)
            def _():
                relay_copy(c, 1, 2).start()

            @pl.when(lax.rem(c, 2) == 1)
            def _():
                relay_copy(c, 2, 1).start()

        input_share(c)

        @pl.when(c > 0)
        def _():
            weight_share(c - 1)

    def h_copy(step):
        return remote(
            gx_acc.at[pl.ds(pl.multiple_of(head_peer(step) * half, half), half)],
            gx_recv.at[step - 1], h_ss.at[step - 1], h_rs.at[step - 1],
            {"head": head_peer(step)},
        )

    for step in range(1, n_head):
        h_copy(step).start()
    weight_share(chunks - 1)
    for step in range(1, n_head):
        h_copy(step).wait()
    total = gx_acc[pl.ds(pl.multiple_of(me_head * half, half), half)]
    for step in range(1, n_head):
        total = total + gx_recv[step - 1]
    gx_ref[...] = total.astype(gx_ref.dtype)

    @pl.loop(0, chunks)
    def _(c):
        for step in range(1, n_seq):
            z_copy(c, step).wait()
        share = gw_ref[c // parts, :, cols(c)]
        for step in range(1, n_seq):
            share = share + z_recv[c, step - 1].astype(jnp.float32)
        gw_ref[c // parts, :, cols(c)] = share
        for step in direct:
            dp_copy(c, step).wait_send()
        if relay:
            relay_copy(c, 1, 2).wait_send()


def grads(d_chunks, lat_t, w_three):
    n_dp, n_seq, n_head = (lax.axis_size(axis) for axis in ("dp", "seq", "head"))
    chunks, slab, width = d_chunks.shape
    three, model_width, head_width = w_three.shape
    rows = model_width // (n_dp * n_seq)
    half = slab // n_head
    vmem = pl.BlockSpec(memory_space=pltpu.VMEM)
    dma = pltpu.SemaphoreType.DMA
    return pl.pallas_call(
        functools.partial(grads_kernel, n_dp, n_seq, n_head),
        out_shape=(
            jax.ShapeDtypeStruct((three, rows, head_width), jnp.float32),
            jax.ShapeDtypeStruct((half, model_width), jnp.bfloat16),
        ),
        in_specs=[vmem, vmem, pl.BlockSpec(memory_space=pl.ANY)],
        out_specs=(vmem, vmem),
        scratch_shapes=[
            pltpu.VMEM((chunks, n_dp - 1, slab, width), jnp.bfloat16),
            pltpu.VMEM((chunks, model_width, width), jnp.bfloat16),
            pltpu.VMEM((n_seq, rows, width), jnp.float32),
            pltpu.VMEM((chunks, n_seq, rows, width), jnp.bfloat16),
            pltpu.VMEM((chunks, n_seq - 1, rows, width), jnp.bfloat16),
            pltpu.VMEM((slab, model_width), jnp.float32),
            pltpu.VMEM((n_head - 1, half, model_width), jnp.float32),
            dma((chunks,)),
            dma((chunks, n_dp - 1)),
            dma((chunks, n_dp - 1)),
            dma((chunks, n_seq - 1)),
            dma((chunks, n_seq - 1)),
            dma((n_head - 1,)),
            dma((n_head - 1,)),
        ],
        compiler_params=pltpu.CompilerParams(
            collective_id=0, has_side_effects=True, vmem_limit_bytes=60 * 1024 * 1024
        ),
        name="grads",
    )(d_chunks, lat_t, w_three)


def layer_kernel(
    n_dp, n_seq, n_head, lat_ref, w_ref, qg_ref, kg_ref, near_ref, do_ref,
    out_ref, d_ref, latt_ref,
    lat_buf, w_buf, do_buf, q_raw, k_raw, q_hat, k_hat, v_hat, mask, mask_t, stat, stat_t, clip_buf,
    l_sem, w_sem, a_ss, a_rs, f_ss, f_rs, o_ss, o_rs, s_ss, s_rs, c_ss, c_rs,
):
    three, model_width, head_width = w_ref.shape
    slab = lat_ref.shape[0]
    chunks, _, width = d_ref.shape
    parts = chunks // three
    group = width // HD
    heads = head_width // HD
    half = slab // n_head
    block = model_width // n_dp
    scale = 1.0 / math.sqrt(HD)
    me_dp = lax.axis_index("dp")
    me_seq = lax.axis_index("seq")
    me_head = lax.axis_index("head")
    below = me_seq > 0
    above = me_seq < n_seq - 1

    def dp_peer(step, sign=1):
        if n_dp == 4:
            low, high = lax.rem(me_dp, 2), me_dp // 2
            if step % 2:
                low = 1 - low
            if step // 2:
                high = 1 - high
            return high * 2 + low
        return lax.rem(me_dp + n_dp + sign * step, n_dp)

    def head_peer(step, sign=1):
        return lax.rem(me_head + n_head + sign * step, n_head)

    own_lat = pltpu.make_async_copy(lat_ref, lat_buf.at[1], l_sem.at[0])
    own_do = pltpu.make_async_copy(do_ref, do_buf.at[1], l_sem.at[1])

    def cols(p):
        return pl.ds(pl.multiple_of(p * width, width), width)

    def w_copy(c):
        at = cols(lax.rem(c, parts))
        return pltpu.make_async_copy(
            w_ref.at[c // parts, :, at], w_buf.at[c // parts, :, at], w_sem.at[c]
        )

    own_lat.start()

    @pl.loop(0, chunks)
    def _(c):
        w_copy(c).start()

    own_do.start()

    barrier = pltpu.get_barrier_semaphore()

    @pl.when(below)
    def _():
        pl.semaphore_signal(barrier, inc=1, device_id={"seq": me_seq - 1}, device_id_type=MESH)

    @pl.when(above)
    def _():
        pl.semaphore_signal(barrier, inc=1, device_id={"seq": me_seq + 1}, device_id_type=MESH)

    for step in range(1, n_dp):
        pl.semaphore_signal(
            barrier, inc=1, device_id={"dp": dp_peer(step, -1)}, device_id_type=MESH
        )
    for step in range(1, n_head):
        pl.semaphore_signal(
            barrier, inc=1, device_id={"head": head_peer(step, -1)}, device_id_type=MESH
        )
    sides = jnp.minimum(me_seq, 1) + jnp.minimum(n_seq - 1 - me_seq, 1)
    pl.semaphore_wait(barrier, n_dp - 1 + n_head - 1 + sides)

    my_rows = pl.ds(pl.multiple_of(me_head * half, half), half)

    def lat_copy(side):
        return remote(
            lat_ref.at[my_rows], lat_buf.at[2 - 2 * side, my_rows],
            a_ss.at[side], a_rs.at[side], {"seq": me_seq + 2 * side - 1},
        )

    def do_copy(side):
        return remote(
            do_ref, do_buf.at[2 - 2 * side],
            o_ss.at[side], o_rs.at[side], {"seq": me_seq + 2 * side - 1},
        )

    def stat_copy(side):
        return remote(
            stat_t.at[1], stat_t.at[2 - 2 * side],
            s_ss.at[side], s_rs.at[side], {"seq": me_seq + 2 * side - 1},
        )

    def pass_copy(slot, step):
        return remote(
            lat_buf.at[slot, my_rows], lat_buf.at[slot, my_rows],
            f_ss.at[slot // 2, step - 1], f_rs.at[slot // 2, step - 1],
            {"head": head_peer(step)},
        )

    def clip_copy(step):
        peer = dp_peer(step)
        return remote(
            lat_ref.at[:, pl.ds(pl.multiple_of(peer * block, block), block)],
            clip_buf.at[step - 1], c_ss.at[step - 1], c_rs.at[step - 1], {"dp": peer},
        )

    @pl.when(below)
    def _():
        lat_copy(0).start()

    @pl.when(above)
    def _():
        lat_copy(1).start()

    for step in range(1, n_dp):
        clip_copy(step).start()

    @pl.when(below)
    def _():
        do_copy(0).start()

    @pl.when(above)
    def _():
        do_copy(1).start()

    def clear(slot):
        lat_buf[slot] = jnp.zeros_like(lat_buf[slot])
        do_buf[slot] = jnp.zeros_like(do_buf[slot])
        stat_t[slot] = jnp.ones_like(stat_t[slot])

    @pl.when(me_seq == 0)
    def _():
        clear(0)

    @pl.when(me_seq == n_seq - 1)
    def _():
        clear(2)

    tiles = near_ref.shape[0]
    near = near_ref[...]
    tile_ids = lax.broadcasted_iota(jnp.int32, (tiles, tiles), 1)
    hits = jnp.zeros((tiles, tiles), jnp.float32)
    for slot in range(near_ref.shape[1]):
        hits = jnp.where(near[:, slot : slot + 1] == tile_ids, 1.0, hits)
    hits = hits.astype(jnp.bfloat16)
    own_tile = me_seq * (slab // TILE)
    first_tile = own_tile - slab // TILE
    own_pick = lax.broadcasted_iota(jnp.int32, (slab, tiles), 1) == (
        lax.broadcasted_iota(jnp.int32, (slab, tiles), 0) // TILE + own_tile
    )
    own_pick = jnp.where(own_pick, 1.0, 0.0).astype(jnp.bfloat16)
    wide_pick = lax.broadcasted_iota(jnp.int32, (tiles, 3 * slab), 0) == (
        lax.broadcasted_iota(jnp.int32, (tiles, 3 * slab), 1) // TILE + first_tile
    )
    wide_pick = jnp.where(wide_pick, 1.0, 0.0).astype(jnp.bfloat16)
    picked = jnp.dot(own_pick, hits, preferred_element_type=jnp.float32).astype(jnp.bfloat16)
    mask[...] = jnp.dot(picked, wide_pick, preferred_element_type=jnp.float32)
    picked = lax.dot_general(
        own_pick, hits, (((1,), (1,)), ((), ())), preferred_element_type=jnp.float32
    ).astype(jnp.bfloat16)
    mask_t[...] = jnp.dot(picked, wide_pick, preferred_element_type=jnp.float32)

    q_gain = qg_ref[...]
    k_gain = kg_ref[...]
    own_lat.wait()

    def arrive(slot, side):
        lat_copy(side).wait_recv()
        for step in range(1, n_head):
            pass_copy(slot, step).start()

    def passed(slot):
        for step in range(1, n_head):
            pass_copy(slot, step).wait_recv()

    @pl.loop(0, 3)
    def _(turn):
        slot = lax.rem(turn + 1, 3)

        @pl.when(turn == 1)
        def _():
            @pl.when(above)
            def _():
                arrive(2, 0)

            @pl.when(below)
            def _():
                arrive(0, 1)

            @pl.when(above)
            def _():
                passed(2)

        @pl.when((turn == 2) & below)
        def _():
            passed(0)

        for kind in range(three):
            @pl.loop(0, parts)
            def _(p):
                @pl.when(turn == 0)
                def _():
                    w_copy(kind * parts + p).wait()

                raw = jnp.dot(
                    lat_buf[slot], w_buf[kind, :, cols(p)], preferred_element_type=jnp.float32
                )
                if kind == 2:
                    v_hat[slot, :, cols(p)] = raw.astype(jnp.bfloat16)
                else:
                    kept, normed, gain = ((q_raw, q_hat, q_gain), (k_raw, k_hat, k_gain))[kind]

                    @pl.when(turn == 0)
                    def _():
                        kept[:, cols(p)] = raw

                    pieces = []
                    for h in range(group):
                        piece = raw[:, h * HD : (h + 1) * HD]
                        pieces.append((piece * inv_rms(piece) * gain).astype(jnp.bfloat16))
                    normed[slot, :, cols(p)] = jnp.concatenate(pieces, axis=1)

    def at(h):
        return pl.ds(pl.multiple_of(h * HD, HD), HD)

    def nt(a, b):
        return lax.dot_general(a, b, (((1,), (1,)), ((), ())), preferred_element_type=jnp.float32)

    def put(kind, h, value):
        d_ref[kind * parts + h // group, :, at(lax.rem(h, group))] = value.astype(jnp.bfloat16)

    own_do.wait()
    lanes = lax.broadcasted_iota(jnp.int32, (slab, 128), 1)
    stat[...] = jnp.zeros_like(stat)

    @pl.loop(0, heads)
    def _(h):
        queries = q_hat[1, :, at(h)]
        keys = k_hat[:, :, at(h)].reshape(3 * slab, HD)
        values = v_hat[:, :, at(h)].reshape(3 * slab, HD)
        expo = jnp.exp(nt(queries, keys) * scale) * mask[...]
        row_total = jnp.sum(expo, axis=-1, keepdims=True)
        probs = expo * (1.0 / row_total)
        out_ref[:, at(h)] = jnp.dot(
            probs.astype(jnp.bfloat16), values, preferred_element_type=jnp.float32
        ).astype(jnp.bfloat16)
        d_probs = nt(do_buf[1, :, at(h)], values)
        row_delta = jnp.sum(probs * d_probs, axis=-1, keepdims=True)
        d_scores = (probs * (d_probs - row_delta) * scale).astype(jnp.bfloat16)
        d_qhat = jnp.dot(d_scores, keys, preferred_element_type=jnp.float32)
        raw = q_raw[:, at(h)]
        put(0, h, norm_back(raw, inv_rms(raw), q_gain, d_qhat))
        rows = jnp.where(lanes == 2 * h, row_total, stat[...])
        stat[...] = jnp.where(lanes == 2 * h + 1, row_delta, rows)

    stat_t[1] = jnp.transpose(stat[...])[: stat_t.shape[1]]

    @pl.when(below)
    def _():
        stat_copy(0).start()

    @pl.when(above)
    def _():
        stat_copy(1).start()

    own_cols = pl.ds(pl.multiple_of(me_dp * block, block), block)
    latt_ref[:, :slab] = jnp.transpose(lat_buf[1, :, own_cols])
    for step in range(1, n_dp):
        clip_copy(step).wait_recv()
        latt_ref[:, step * slab : (step + 1) * slab] = jnp.transpose(clip_buf[step - 1])

    @pl.when(above)
    def _():
        do_copy(0).wait_recv()
        stat_copy(0).wait_recv()

    @pl.when(below)
    def _():
        do_copy(1).wait_recv()
        stat_copy(1).wait_recv()

    @pl.loop(0, heads)
    def _(h):
        keys = k_hat[1, :, at(h)]
        values = v_hat[1, :, at(h)]
        queries = q_hat[:, :, at(h)].reshape(3 * slab, HD)
        upstream = do_buf[:, :, at(h)].reshape(3 * slab, HD)
        total = jnp.concatenate([stat_t[s, pl.ds(2 * h, 1), :] for s in range(3)], axis=1)
        delta = jnp.concatenate([stat_t[s, pl.ds(2 * h + 1, 1), :] for s in range(3)], axis=1)
        probs = jnp.exp(nt(keys, queries) * scale) * mask_t[...] * (1.0 / total)
        put(2, h, jnp.dot(probs.astype(jnp.bfloat16), upstream, preferred_element_type=jnp.float32))
        d_scores = (probs * (nt(values, upstream) - delta) * scale).astype(jnp.bfloat16)
        d_khat = jnp.dot(d_scores, queries, preferred_element_type=jnp.float32)
        raw = k_raw[:, at(h)]
        put(1, h, norm_back(raw, inv_rms(raw), k_gain, d_khat))

    def settle(slot, side):
        lat_copy(side).wait_send()
        do_copy(side).wait_send()
        stat_copy(side).wait_send()
        for step in range(1, n_head):
            pass_copy(slot, step).wait_send()

    @pl.when(below)
    def _():
        settle(0, 0)

    @pl.when(above)
    def _():
        settle(2, 1)

    for step in range(1, n_dp):
        clip_copy(step).wait_send()


def layer(slab_tokens, w_three, q_gain, k_gain, neighbours, upstream):
    n_dp, n_seq, n_head = (lax.axis_size(axis) for axis in ("dp", "seq", "head"))
    slab = slab_tokens.shape[0]
    three, model_width, head_width = w_three.shape
    heads = head_width // HD
    group = 3 if heads % 3 == 0 else 1
    width = group * HD
    chunks = three * heads // group
    block = model_width // n_dp
    stat_rows = -(-2 * heads // 8) * 8
    vmem = pl.BlockSpec(memory_space=pltpu.VMEM)
    anywhere = pl.BlockSpec(memory_space=pl.ANY)
    dma = pltpu.SemaphoreType.DMA
    bf16, f32 = jnp.bfloat16, jnp.float32
    return pl.pallas_call(
        functools.partial(layer_kernel, n_dp, n_seq, n_head),
        out_shape=(
            jax.ShapeDtypeStruct((slab, head_width), bf16),
            jax.ShapeDtypeStruct((chunks, slab, width), bf16),
            jax.ShapeDtypeStruct((block, n_dp * slab), bf16),
        ),
        in_specs=[anywhere, anywhere, vmem, vmem, vmem, anywhere],
        out_specs=(vmem, vmem, vmem),
        scratch_shapes=[
            pltpu.VMEM((3, slab, model_width), bf16),
            pltpu.VMEM((three, model_width, head_width), bf16),
            pltpu.VMEM((3, slab, head_width), bf16),
            pltpu.VMEM((slab, head_width), f32),
            pltpu.VMEM((slab, head_width), f32),
            pltpu.VMEM((3, slab, head_width), bf16),
            pltpu.VMEM((3, slab, head_width), bf16),
            pltpu.VMEM((3, slab, head_width), bf16),
            pltpu.VMEM((slab, 3 * slab), f32),
            pltpu.VMEM((slab, 3 * slab), f32),
            pltpu.VMEM((slab, 128), f32),
            pltpu.VMEM((3, stat_rows, slab), f32),
            pltpu.VMEM((n_dp - 1, slab, block), bf16),
            dma((2,)),
            dma((chunks,)),
            dma((2,)),
            dma((2,)),
            dma((2, n_head - 1)),
            dma((2, n_head - 1)),
            dma((2,)),
            dma((2,)),
            dma((2,)),
            dma((2,)),
            dma((n_dp - 1,)),
            dma((n_dp - 1,)),
        ],
        compiler_params=pltpu.CompilerParams(
            collective_id=1, has_side_effects=True, vmem_limit_bytes=60 * 1024 * 1024
        ),
        name="layer",
    )(slab_tokens, w_three, q_gain.reshape(1, HD), k_gain.reshape(1, HD), neighbours, upstream)


def local(latents, w_qkv, q_gain, k_gain, neighbours, grad_out):
    w_three = jnp.transpose(w_qkv, (1, 0, 2))
    attn_out, d_chunks, lat_t = layer(
        latents[0], w_three, q_gain, k_gain, neighbours, grad_out[0]
    )
    share, grad_rows = grads(d_chunks, lat_t, w_three)
    return (attn_out[None], grad_rows[None], jnp.transpose(share, (1, 0, 2)))


def solution(mesh):
    in_specs = (P("dp", "seq", None), P(None, None, "head"), P(), P(), P(), P("dp", "seq", "head"))
    out_specs = (
        P("dp", "seq", "head"),
        P("dp", ("seq", "head"), None),
        P(("dp", "seq"), None, "head"),
    )
    return jax.shard_map(local, mesh=mesh, in_specs=in_specs, out_specs=out_specs, check_vma=False)
```

```python
import functools
import math

import jax
import jax.numpy as jnp
from jax import lax
from jax.experimental import pallas as pl
from jax.experimental.pallas import tpu as pltpu
from jax.sharding import PartitionSpec as P

MESH = pl.DeviceIdType.MESH

HD = 128
TILE = 64


EPS = 1e-06


def inv_rms(values):
    return lax.rsqrt(jnp.mean(values * values, axis=-1, keepdims=True) + EPS)


def norm_back(raw, inverse, gain, upstream):
    normed = raw * inverse
    weighted = upstream * gain
    return inverse * (weighted - normed * jnp.mean(weighted * normed, axis=-1, keepdims=True))


def remote(src, dst, send_sem, recv_sem, peer):
    return pltpu.make_async_remote_copy(
        src_ref=src,
        dst_ref=dst,
        send_sem=send_sem,
        recv_sem=recv_sem,
        device_id=peer,
        device_id_type=MESH,
    )


def layer_kernel(
    n_dp, n_seq, n_head, lat_ref, w_ref, qg_ref, kg_ref, near_ref, do_ref,
    out_ref, gw_ref, gx_ref,
    d_ref, latt_ref, gath, part, z_send, z_recv, gx_acc, gx_recv, lat_buf, w_buf, do_buf, q_raw, k_raw, q_hat, k_hat, v_hat, mask, mask_t, stat, stat_t, clip_buf,
    l_sem, w_sem, a_ss, a_rs, f_ss, f_rs, o_ss, o_rs, s_ss, s_rs, c_ss, c_rs,
    d_ss, d_rs, z_ss, z_rs, h_ss, h_rs,
):
    three, model_width, head_width = w_ref.shape
    slab = lat_ref.shape[0]
    chunks, _, width = d_ref.shape
    parts = chunks // three
    group = width // HD
    heads = head_width // HD
    half = slab // n_head
    block = model_width // n_dp
    scale = 1.0 / math.sqrt(HD)
    me_dp = lax.axis_index("dp")
    me_seq = lax.axis_index("seq")
    me_head = lax.axis_index("head")
    below = me_seq > 0
    above = me_seq < n_seq - 1

    def dp_peer(step, sign=1):
        if n_dp == 4:
            low, high = lax.rem(me_dp, 2), me_dp // 2
            if step % 2:
                low = 1 - low
            if step // 2:
                high = 1 - high
            return high * 2 + low
        return lax.rem(me_dp + n_dp + sign * step, n_dp)

    def head_peer(step, sign=1):
        return lax.rem(me_head + n_head + sign * step, n_head)

    own_lat = pltpu.make_async_copy(lat_ref, lat_buf.at[1], l_sem.at[0])
    own_do = pltpu.make_async_copy(do_ref, do_buf.at[1], l_sem.at[1])

    def cols(p):
        return pl.ds(pl.multiple_of(p * width, width), width)

    def w_copy(c):
        at = cols(lax.rem(c, parts))
        return pltpu.make_async_copy(
            w_ref.at[c // parts, :, at], w_buf.at[c // parts, :, at], w_sem.at[c]
        )

    own_lat.start()

    @pl.loop(0, chunks)
    def _(c):
        w_copy(c).start()

    own_do.start()

    def seq_peer(step):
        return lax.rem(me_seq + step, n_seq)

    barrier = pltpu.get_barrier_semaphore()
    for step in range(1, n_seq):
        pl.semaphore_signal(
            barrier, inc=1, device_id={"seq": seq_peer(step)}, device_id_type=MESH
        )
    for step in range(1, n_dp):
        pl.semaphore_signal(
            barrier, inc=1, device_id={"dp": dp_peer(step, -1)}, device_id_type=MESH
        )
    for step in range(1, n_head):
        pl.semaphore_signal(
            barrier, inc=1, device_id={"head": head_peer(step, -1)}, device_id_type=MESH
        )
    pl.semaphore_wait(barrier, n_seq - 1 + n_dp - 1 + n_head - 1)

    my_rows = pl.ds(pl.multiple_of(me_head * half, half), half)

    def lat_copy(side):
        return remote(
            lat_ref.at[my_rows], lat_buf.at[2 - 2 * side, my_rows],
            a_ss.at[side], a_rs.at[side], {"seq": me_seq + 2 * side - 1},
        )

    def do_copy(side):
        return remote(
            do_ref, do_buf.at[2 - 2 * side],
            o_ss.at[side], o_rs.at[side], {"seq": me_seq + 2 * side - 1},
        )

    def stat_copy(side):
        return remote(
            stat_t.at[1], stat_t.at[2 - 2 * side],
            s_ss.at[side], s_rs.at[side], {"seq": me_seq + 2 * side - 1},
        )

    def pass_copy(slot, step):
        return remote(
            lat_buf.at[slot, my_rows], lat_buf.at[slot, my_rows],
            f_ss.at[slot // 2, step - 1], f_rs.at[slot // 2, step - 1],
            {"head": head_peer(step)},
        )

    def clip_copy(step):
        peer = dp_peer(step)
        return remote(
            lat_ref.at[:, pl.ds(pl.multiple_of(peer * block, block), block)],
            clip_buf.at[step - 1], c_ss.at[step - 1], c_rs.at[step - 1], {"dp": peer},
        )

    @pl.when(below)
    def _():
        lat_copy(0).start()

    @pl.when(above)
    def _():
        lat_copy(1).start()

    for step in range(1, n_dp):
        clip_copy(step).start()

    @pl.when(below)
    def _():
        do_copy(0).start()

    @pl.when(above)
    def _():
        do_copy(1).start()

    def clear(slot):
        lat_buf[slot] = jnp.zeros_like(lat_buf[slot])
        do_buf[slot] = jnp.zeros_like(do_buf[slot])
        stat_t[slot] = jnp.ones_like(stat_t[slot])

    @pl.when(me_seq == 0)
    def _():
        clear(0)

    @pl.when(me_seq == n_seq - 1)
    def _():
        clear(2)

    tiles = near_ref.shape[0]
    near = near_ref[...]
    tile_ids = lax.broadcasted_iota(jnp.int32, (tiles, tiles), 1)
    hits = jnp.zeros((tiles, tiles), jnp.float32)
    for slot in range(near_ref.shape[1]):
        hits = jnp.where(near[:, slot : slot + 1] == tile_ids, 1.0, hits)
    hits = hits.astype(jnp.bfloat16)
    own_tile = me_seq * (slab // TILE)
    first_tile = own_tile - slab // TILE
    own_pick = lax.broadcasted_iota(jnp.int32, (slab, tiles), 1) == (
        lax.broadcasted_iota(jnp.int32, (slab, tiles), 0) // TILE + own_tile
    )
    own_pick = jnp.where(own_pick, 1.0, 0.0).astype(jnp.bfloat16)
    wide_pick = lax.broadcasted_iota(jnp.int32, (tiles, 3 * slab), 0) == (
        lax.broadcasted_iota(jnp.int32, (tiles, 3 * slab), 1) // TILE + first_tile
    )
    wide_pick = jnp.where(wide_pick, 1.0, 0.0).astype(jnp.bfloat16)
    picked = jnp.dot(own_pick, hits, preferred_element_type=jnp.float32).astype(jnp.bfloat16)
    mask[...] = jnp.dot(picked, wide_pick, preferred_element_type=jnp.float32)
    picked = lax.dot_general(
        own_pick, hits, (((1,), (1,)), ((), ())), preferred_element_type=jnp.float32
    ).astype(jnp.bfloat16)
    mask_t[...] = jnp.dot(picked, wide_pick, preferred_element_type=jnp.float32)

    q_gain = qg_ref[...]
    k_gain = kg_ref[...]
    own_lat.wait()

    def arrive(slot, side):
        lat_copy(side).wait_recv()
        for step in range(1, n_head):
            pass_copy(slot, step).start()

    def passed(slot):
        for step in range(1, n_head):
            pass_copy(slot, step).wait_recv()

    @pl.loop(0, 3)
    def _(turn):
        slot = lax.rem(turn + 1, 3)

        @pl.when(turn == 1)
        def _():
            @pl.when(above)
            def _():
                arrive(2, 0)

            @pl.when(below)
            def _():
                arrive(0, 1)

            @pl.when(above)
            def _():
                passed(2)

        @pl.when((turn == 2) & below)
        def _():
            passed(0)

        for kind in range(three):
            @pl.loop(0, parts)
            def _(p):
                @pl.when(turn == 0)
                def _():
                    w_copy(kind * parts + p).wait()

                raw = jnp.dot(
                    lat_buf[slot], w_buf[kind, :, cols(p)], preferred_element_type=jnp.float32
                )
                if kind == 2:
                    v_hat[slot, :, cols(p)] = raw.astype(jnp.bfloat16)
                else:
                    kept, normed, gain = ((q_raw, q_hat, q_gain), (k_raw, k_hat, k_gain))[kind]

                    @pl.when(turn == 0)
                    def _():
                        kept[:, cols(p)] = raw

                    pieces = []
                    for h in range(group):
                        piece = raw[:, h * HD : (h + 1) * HD]
                        pieces.append((piece * inv_rms(piece) * gain).astype(jnp.bfloat16))
                    normed[slot, :, cols(p)] = jnp.concatenate(pieces, axis=1)

    def at(h):
        return pl.ds(pl.multiple_of(h * HD, HD), HD)

    def nt(a, b):
        return lax.dot_general(a, b, (((1,), (1,)), ((), ())), preferred_element_type=jnp.float32)

    def put(position, h, value):
        d_ref[position, :, at(lax.rem(h, group))] = value.astype(jnp.bfloat16)

    def place(position):
        late = jnp.maximum(position - parts, 0)
        is_late = jnp.where(position >= parts, 1, 0)
        kind = is_late * (1 + lax.rem(late, 2))
        p = is_late * (late // 2) + (1 - is_late) * position
        return kind, cols(p)

    relay = n_dp == 4
    direct = (1, 2) if relay else tuple(range(1, n_dp))
    rows = gw_ref.shape[1]

    def dp_copy(c, step):
        return remote(
            d_ref.at[c], gath.at[c, step - 1],
            d_ss.at[c, step - 1], d_rs.at[c, step - 1], {"dp": dp_peer(step)},
        )

    def relay_copy(c, via, onward):
        return remote(
            gath.at[c, via - 1], gath.at[c, 2],
            d_ss.at[c, 2], d_rs.at[c, 2], {"dp": dp_peer(onward)},
        )

    def z_copy(c, step):
        return remote(
            z_send.at[c, seq_peer(step)], z_recv.at[c, step - 1],
            z_ss.at[c, step - 1], z_rs.at[c, step - 1], {"seq": seq_peer(step)},
        )

    def send_own(c):
        for step in direct:
            dp_copy(c, step).start()

    def pass_on(c):
        for step in direct:
            dp_copy(c, step).wait_recv()
        if relay:
            @pl.when(lax.rem(c, 2) == 0)
            def _():
                relay_copy(c, 1, 2).start()

            @pl.when(lax.rem(c, 2) == 1)
            def _():
                relay_copy(c, 2, 1).start()

    def input_share(c):
        kind, where = place(c)
        gx_acc[...] += nt(d_ref[c], w_buf[kind, :, where])

    def weight_share(c):
        if relay:
            relay_copy(c, 1, 2).wait_recv()
        others = gath[c].reshape((n_dp - 1) * slab, width)
        product = jnp.dot(latt_ref[:, :slab], d_ref[c], preferred_element_type=jnp.float32)
        product += jnp.dot(latt_ref[:, slab:], others, preferred_element_type=jnp.float32)
        product = product.reshape(n_seq, rows, width)
        part[...] = product
        z_send[c] = product.astype(jnp.bfloat16)
        for step in range(n_seq - 1, 0, -1):
            z_copy(c, step).start()
        kind, where = place(c)
        gw_ref[kind, :, where] = part[me_seq]

    own_do.wait()
    lanes = lax.broadcasted_iota(jnp.int32, (slab, 128), 1)
    stat[...] = jnp.zeros_like(stat)

    @pl.loop(0, heads)
    def _(h):
        queries = q_hat[1, :, at(h)]
        keys = k_hat[:, :, at(h)].reshape(3 * slab, HD)
        values = v_hat[:, :, at(h)].reshape(3 * slab, HD)
        expo = jnp.exp(nt(queries, keys) * scale) * mask[...]
        row_total = jnp.sum(expo, axis=-1, keepdims=True)
        probs = expo * (1.0 / row_total)
        out_ref[:, at(h)] = jnp.dot(
            probs.astype(jnp.bfloat16), values, preferred_element_type=jnp.float32
        ).astype(jnp.bfloat16)
        d_probs = nt(do_buf[1, :, at(h)], values)
        row_delta = jnp.sum(probs * d_probs, axis=-1, keepdims=True)
        d_scores = (probs * (d_probs - row_delta) * scale).astype(jnp.bfloat16)
        d_qhat = jnp.dot(d_scores, keys, preferred_element_type=jnp.float32)
        raw = q_raw[:, at(h)]
        put(h // group, h, norm_back(raw, inv_rms(raw), q_gain, d_qhat))
        rows = jnp.where(lanes == 2 * h, row_total, stat[...])
        stat[...] = jnp.where(lanes == 2 * h + 1, row_delta, rows)

        @pl.when(lax.rem(h, group) == group - 1)
        def _():
            send_own(h // group)

    stat_t[1] = jnp.transpose(stat[...])[: stat_t.shape[1]]

    @pl.when(below)
    def _():
        stat_copy(0).start()

    @pl.when(above)
    def _():
        stat_copy(1).start()

    own_cols = pl.ds(pl.multiple_of(me_dp * block, block), block)
    latt_ref[:, :slab] = jnp.transpose(lat_buf[1, :, own_cols])
    for step in range(1, n_dp):
        clip_copy(step).wait_recv()
        latt_ref[:, step * slab : (step + 1) * slab] = jnp.transpose(clip_buf[step - 1])

    @pl.when(above)
    def _():
        do_copy(0).wait_recv()
        stat_copy(0).wait_recv()

    @pl.when(below)
    def _():
        do_copy(1).wait_recv()
        stat_copy(1).wait_recv()

    gx_acc[...] = jnp.zeros_like(gx_acc)

    def reverse(h):
        keys = k_hat[1, :, at(h)]
        values = v_hat[1, :, at(h)]
        queries = q_hat[:, :, at(h)].reshape(3 * slab, HD)
        upstream = do_buf[:, :, at(h)].reshape(3 * slab, HD)
        total = jnp.concatenate([stat_t[s, pl.ds(2 * h, 1), :] for s in range(3)], axis=1)
        delta = jnp.concatenate([stat_t[s, pl.ds(2 * h + 1, 1), :] for s in range(3)], axis=1)
        probs = jnp.exp(nt(keys, queries) * scale) * mask_t[...] * (1.0 / total)
        late = parts + 2 * (h // group)
        put(late + 1, h, jnp.dot(probs.astype(jnp.bfloat16), upstream, preferred_element_type=jnp.float32))
        d_scores = (probs * (nt(values, upstream) - delta) * scale).astype(jnp.bfloat16)
        d_khat = jnp.dot(d_scores, queries, preferred_element_type=jnp.float32)
        raw = k_raw[:, at(h)]
        put(late, h, norm_back(raw, inv_rms(raw), k_gain, d_khat))

    @pl.loop(0, chunks)
    def _(tick):
        @pl.when(tick > 0)
        def _():
            weight_share(tick - 1)

        @pl.when(tick < parts)
        def _():
            @pl.loop(0, group)
            def _(h):
                reverse(tick * group + h)

        pass_on(tick)

        @pl.when(tick < chunks - parts)
        def _():
            send_own(tick + parts)

        input_share(tick)

    share = gx_ref.shape[0]

    def h_copy(step):
        peer = head_peer(step)
        return remote(
            gx_acc.at[pl.ds(pl.multiple_of(peer * share, share), share)],
            gx_recv.at[step - 1], h_ss.at[step - 1], h_rs.at[step - 1], {"head": peer},
        )

    for step in range(1, n_head):
        h_copy(step).start()
    weight_share(chunks - 1)
    for step in range(1, n_head):
        h_copy(step).wait()
    total = gx_acc[pl.ds(pl.multiple_of(me_head * share, share), share)]
    for step in range(1, n_head):
        total = total + gx_recv[step - 1]
    gx_ref[...] = total.astype(gx_ref.dtype)

    @pl.loop(0, chunks)
    def _(c):
        for step in range(1, n_seq):
            z_copy(c, step).wait()
        kind, where = place(c)
        summed = gw_ref[kind, :, where]
        for step in range(1, n_seq):
            summed = summed + z_recv[c, step - 1].astype(jnp.float32)
        gw_ref[kind, :, where] = summed
        for step in direct:
            dp_copy(c, step).wait_send()
        if relay:
            relay_copy(c, 1, 2).wait_send()

    def settle(slot, side):
        lat_copy(side).wait_send()
        do_copy(side).wait_send()
        stat_copy(side).wait_send()
        for step in range(1, n_head):
            pass_copy(slot, step).wait_send()

    @pl.when(below)
    def _():
        settle(0, 0)

    @pl.when(above)
    def _():
        settle(2, 1)

    for step in range(1, n_dp):
        clip_copy(step).wait_send()


def layer(slab_tokens, w_three, q_gain, k_gain, neighbours, upstream):
    n_dp, n_seq, n_head = (lax.axis_size(axis) for axis in ("dp", "seq", "head"))
    slab = slab_tokens.shape[0]
    three, model_width, head_width = w_three.shape
    heads = head_width // HD
    group = 3 if heads % 3 == 0 else 1
    width = group * HD
    chunks = three * heads // group
    block = model_width // n_dp
    rows = block // n_seq
    share = slab // n_head
    stat_rows = -(-2 * heads // 8) * 8
    vmem = pl.BlockSpec(memory_space=pltpu.VMEM)
    anywhere = pl.BlockSpec(memory_space=pl.ANY)
    dma = pltpu.SemaphoreType.DMA
    bf16, f32 = jnp.bfloat16, jnp.float32
    return pl.pallas_call(
        functools.partial(layer_kernel, n_dp, n_seq, n_head),
        out_shape=(
            jax.ShapeDtypeStruct((slab, head_width), bf16),
            jax.ShapeDtypeStruct((three, rows, head_width), f32),
            jax.ShapeDtypeStruct((share, model_width), bf16),
        ),
        in_specs=[anywhere, anywhere, vmem, vmem, vmem, anywhere],
        out_specs=(vmem, vmem, vmem),
        scratch_shapes=[
            pltpu.VMEM((chunks, slab, width), bf16),
            pltpu.VMEM((block, n_dp * slab), bf16),
            pltpu.VMEM((chunks, n_dp - 1, slab, width), bf16),
            pltpu.VMEM((n_seq, rows, width), f32),
            pltpu.VMEM((chunks, n_seq, rows, width), bf16),
            pltpu.VMEM((chunks, n_seq - 1, rows, width), bf16),
            pltpu.VMEM((slab, model_width), f32),
            pltpu.VMEM((n_head - 1, share, model_width), f32),
            pltpu.VMEM((3, slab, model_width), bf16),
            pltpu.VMEM((three, model_width, head_width), bf16),
            pltpu.VMEM((3, slab, head_width), bf16),
            pltpu.VMEM((slab, head_width), f32),
            pltpu.VMEM((slab, head_width), f32),
            pltpu.VMEM((3, slab, head_width), bf16),
            pltpu.VMEM((3, slab, head_width), bf16),
            pltpu.VMEM((3, slab, head_width), bf16),
            pltpu.VMEM((slab, 3 * slab), f32),
            pltpu.VMEM((slab, 3 * slab), f32),
            pltpu.VMEM((slab, 128), f32),
            pltpu.VMEM((3, stat_rows, slab), f32),
            pltpu.VMEM((n_dp - 1, slab, block), bf16),
            dma((2,)),
            dma((chunks,)),
            dma((2,)),
            dma((2,)),
            dma((2, n_head - 1)),
            dma((2, n_head - 1)),
            dma((2,)),
            dma((2,)),
            dma((2,)),
            dma((2,)),
            dma((n_dp - 1,)),
            dma((n_dp - 1,)),
            dma((chunks, n_dp - 1)),
            dma((chunks, n_dp - 1)),
            dma((chunks, n_seq - 1)),
            dma((chunks, n_seq - 1)),
            dma((n_head - 1,)),
            dma((n_head - 1,)),
        ],
        compiler_params=pltpu.CompilerParams(
            collective_id=0, has_side_effects=True, vmem_limit_bytes=60 * 1024 * 1024
        ),
        name="layer",
    )(slab_tokens, w_three, q_gain.reshape(1, HD), k_gain.reshape(1, HD), neighbours, upstream)


def local(latents, w_qkv, q_gain, k_gain, neighbours, grad_out):
    w_three = jnp.transpose(w_qkv, (1, 0, 2))
    attn_out, grad_w, grad_x = layer(
        latents[0], w_three, q_gain, k_gain, neighbours, grad_out[0]
    )
    return (attn_out[None], grad_x[None], jnp.transpose(grad_w, (1, 0, 2)))


def solution(mesh):
    in_specs = (P("dp", "seq", None), P(None, None, "head"), P(), P(), P(), P("dp", "seq", "head"))
    out_specs = (
        P("dp", "seq", "head"),
        P("dp", ("seq", "head"), None),
        P(("dp", "seq"), None, "head"),
    )
    return jax.shard_map(local, mesh=mesh, in_specs=in_specs, out_specs=out_specs, check_vma=False)
```

```python
import functools
import math

import jax
import jax.numpy as jnp
from jax import lax
from jax.experimental import pallas as pl
from jax.experimental.pallas import tpu as pltpu
from jax.sharding import PartitionSpec as P

MESH = pl.DeviceIdType.MESH

HD = 128
TILE = 64


EPS = 1e-06


def inv_rms(values):
    return lax.rsqrt(jnp.mean(values * values, axis=-1, keepdims=True) + EPS)


def norm_back(raw, inverse, gain, upstream):
    normed = raw * inverse
    weighted = upstream * gain
    return inverse * (weighted - normed * jnp.mean(weighted * normed, axis=-1, keepdims=True))


def remote(src, dst, send_sem, recv_sem, peer):
    return pltpu.make_async_remote_copy(
        src_ref=src,
        dst_ref=dst,
        send_sem=send_sem,
        recv_sem=recv_sem,
        device_id=peer,
        device_id_type=MESH,
    )


def layer_kernel(
    n_dp, n_seq, n_head, lat_ref, w_ref, qg_ref, kg_ref, near_ref, do_ref,
    out_ref, gw_ref, gx_ref,
    d_ref, latt_ref, gath, part, flow, gx_acc, gx_recv, lat_buf, w_buf, do_buf, q_raw, k_raw, q_hat, k_hat, v_hat, mask, mask_t, stat, stat_t, clip_buf,
    l_sem, w_sem, a_ss, a_rs, f_ss, f_rs, o_ss, o_rs, s_ss, s_rs, c_ss, c_rs,
    d_ss, d_rs, z_ss, z_rs, h_ss, h_rs,
):
    three, model_width, head_width = w_ref.shape
    slab = lat_ref.shape[0]
    chunks, _, width = d_ref.shape
    parts = chunks // three
    group = width // HD
    heads = head_width // HD
    half = slab // n_head
    block = model_width // n_dp
    scale = 1.0 / math.sqrt(HD)
    me_dp = lax.axis_index("dp")
    me_seq = lax.axis_index("seq")
    me_head = lax.axis_index("head")
    below = me_seq > 0
    above = me_seq < n_seq - 1

    def dp_peer(step, sign=1):
        if n_dp == 4:
            low, high = lax.rem(me_dp, 2), me_dp // 2
            if step % 2:
                low = 1 - low
            if step // 2:
                high = 1 - high
            return high * 2 + low
        return lax.rem(me_dp + n_dp + sign * step, n_dp)

    def head_peer(step, sign=1):
        return lax.rem(me_head + n_head + sign * step, n_head)

    own_lat = pltpu.make_async_copy(lat_ref, lat_buf.at[1], l_sem.at[0])
    own_do = pltpu.make_async_copy(do_ref, do_buf.at[1], l_sem.at[1])

    def cols(p):
        return pl.ds(pl.multiple_of(p * width, width), width)

    def w_copy(c):
        at = cols(lax.rem(c, parts))
        return pltpu.make_async_copy(
            w_ref.at[c // parts, :, at], w_buf.at[c // parts, :, at], w_sem.at[c]
        )

    own_lat.start()

    @pl.loop(0, chunks)
    def _(c):
        w_copy(c).start()

    own_do.start()

    barrier = pltpu.get_barrier_semaphore()

    @pl.when(below)
    def _():
        pl.semaphore_signal(barrier, inc=1, device_id={"seq": me_seq - 1}, device_id_type=MESH)

    @pl.when(above)
    def _():
        pl.semaphore_signal(barrier, inc=1, device_id={"seq": me_seq + 1}, device_id_type=MESH)

    for step in range(1, n_dp):
        pl.semaphore_signal(
            barrier, inc=1, device_id={"dp": dp_peer(step, -1)}, device_id_type=MESH
        )
    for step in range(1, n_head):
        pl.semaphore_signal(
            barrier, inc=1, device_id={"head": head_peer(step, -1)}, device_id_type=MESH
        )
    sides = jnp.minimum(me_seq, 1) + jnp.minimum(n_seq - 1 - me_seq, 1)
    pl.semaphore_wait(barrier, n_dp - 1 + n_head - 1 + sides)

    my_rows = pl.ds(pl.multiple_of(me_head * half, half), half)

    def lat_copy(side):
        return remote(
            lat_ref.at[my_rows], lat_buf.at[2 - 2 * side, my_rows],
            a_ss.at[side], a_rs.at[side], {"seq": me_seq + 2 * side - 1},
        )

    def do_copy(side):
        return remote(
            do_ref, do_buf.at[2 - 2 * side],
            o_ss.at[side], o_rs.at[side], {"seq": me_seq + 2 * side - 1},
        )

    def stat_copy(side):
        return remote(
            stat_t.at[1], stat_t.at[2 - 2 * side],
            s_ss.at[side], s_rs.at[side], {"seq": me_seq + 2 * side - 1},
        )

    def pass_copy(slot, step):
        return remote(
            lat_buf.at[slot, my_rows], lat_buf.at[slot, my_rows],
            f_ss.at[slot // 2, step - 1], f_rs.at[slot // 2, step - 1],
            {"head": head_peer(step)},
        )

    def clip_copy(step):
        peer = dp_peer(step)
        return remote(
            lat_ref.at[:, pl.ds(pl.multiple_of(peer * block, block), block)],
            clip_buf.at[step - 1], c_ss.at[step - 1], c_rs.at[step - 1], {"dp": peer},
        )

    @pl.when(below)
    def _():
        lat_copy(0).start()

    @pl.when(above)
    def _():
        lat_copy(1).start()

    for step in range(1, n_dp):
        clip_copy(step).start()

    @pl.when(below)
    def _():
        do_copy(0).start()

    @pl.when(above)
    def _():
        do_copy(1).start()

    def clear(slot):
        lat_buf[slot] = jnp.zeros_like(lat_buf[slot])
        do_buf[slot] = jnp.zeros_like(do_buf[slot])
        stat_t[slot] = jnp.ones_like(stat_t[slot])

    @pl.when(me_seq == 0)
    def _():
        clear(0)

    @pl.when(me_seq == n_seq - 1)
    def _():
        clear(2)

    tiles = near_ref.shape[0]
    near = near_ref[...]
    tile_ids = lax.broadcasted_iota(jnp.int32, (tiles, tiles), 1)
    hits = jnp.zeros((tiles, tiles), jnp.float32)
    for slot in range(near_ref.shape[1]):
        hits = jnp.where(near[:, slot : slot + 1] == tile_ids, 1.0, hits)
    hits = hits.astype(jnp.bfloat16)
    own_tile = me_seq * (slab // TILE)
    first_tile = own_tile - slab // TILE
    own_pick = lax.broadcasted_iota(jnp.int32, (slab, tiles), 1) == (
        lax.broadcasted_iota(jnp.int32, (slab, tiles), 0) // TILE + own_tile
    )
    own_pick = jnp.where(own_pick, 1.0, 0.0).astype(jnp.bfloat16)
    wide_pick = lax.broadcasted_iota(jnp.int32, (tiles, 3 * slab), 0) == (
        lax.broadcasted_iota(jnp.int32, (tiles, 3 * slab), 1) // TILE + first_tile
    )
    wide_pick = jnp.where(wide_pick, 1.0, 0.0).astype(jnp.bfloat16)
    picked = jnp.dot(own_pick, hits, preferred_element_type=jnp.float32).astype(jnp.bfloat16)
    mask[...] = jnp.dot(picked, wide_pick, preferred_element_type=jnp.float32)
    picked = lax.dot_general(
        own_pick, hits, (((1,), (1,)), ((), ())), preferred_element_type=jnp.float32
    ).astype(jnp.bfloat16)
    mask_t[...] = jnp.dot(picked, wide_pick, preferred_element_type=jnp.float32)

    q_gain = qg_ref[...]
    k_gain = kg_ref[...]
    own_lat.wait()

    def arrive(slot, side):
        lat_copy(side).wait_recv()
        for step in range(1, n_head):
            pass_copy(slot, step).start()

    def passed(slot):
        for step in range(1, n_head):
            pass_copy(slot, step).wait_recv()

    @pl.loop(0, 3)
    def _(turn):
        slot = lax.rem(turn + 1, 3)

        @pl.when(turn == 1)
        def _():
            @pl.when(above)
            def _():
                arrive(2, 0)

            @pl.when(below)
            def _():
                arrive(0, 1)

            @pl.when(above)
            def _():
                passed(2)

        @pl.when((turn == 2) & below)
        def _():
            passed(0)

        for kind in range(three):
            @pl.loop(0, parts)
            def _(p):
                @pl.when(turn == 0)
                def _():
                    w_copy(kind * parts + p).wait()

                raw = jnp.dot(
                    lat_buf[slot], w_buf[kind, :, cols(p)], preferred_element_type=jnp.float32
                )
                if kind == 2:
                    v_hat[slot, :, cols(p)] = raw.astype(jnp.bfloat16)
                else:
                    kept, normed, gain = ((q_raw, q_hat, q_gain), (k_raw, k_hat, k_gain))[kind]

                    @pl.when(turn == 0)
                    def _():
                        kept[:, cols(p)] = raw

                    pieces = []
                    for h in range(group):
                        piece = raw[:, h * HD : (h + 1) * HD]
                        pieces.append((piece * inv_rms(piece) * gain).astype(jnp.bfloat16))
                    normed[slot, :, cols(p)] = jnp.concatenate(pieces, axis=1)

    def at(h):
        return pl.ds(pl.multiple_of(h * HD, HD), HD)

    def nt(a, b):
        return lax.dot_general(a, b, (((1,), (1,)), ((), ())), preferred_element_type=jnp.float32)

    def put(position, h, value):
        d_ref[position, :, at(lax.rem(h, group))] = value.astype(jnp.bfloat16)

    def place(position):
        late = jnp.maximum(position - parts, 0)
        is_late = jnp.where(position >= parts, 1, 0)
        kind = is_late * (1 + lax.rem(late, 2))
        p = is_late * (late // 2) + (1 - is_late) * position
        return kind, cols(p)

    relay = n_dp == 4
    direct = (1, 2) if relay else tuple(range(1, n_dp))
    rows = gw_ref.shape[1]

    def dp_copy(c, step):
        return remote(
            d_ref.at[c], gath.at[c, step - 1],
            d_ss.at[c, step - 1], d_rs.at[c, step - 1], {"dp": dp_peer(step)},
        )

    def relay_copy(c, via, onward):
        return remote(
            gath.at[c, via - 1], gath.at[c, 2],
            d_ss.at[c, 2], d_rs.at[c, 2], {"dp": dp_peer(onward)},
        )

    def hop(side, c, t):
        peer = lax.rem(me_seq + n_seq + 1 - 2 * side, n_seq)
        return remote(
            flow.at[side, c, t], flow.at[side, c, t],
            z_ss.at[side, c, t], z_rs.at[side, c, t], {"seq": peer},
        )

    fed = (below, above)

    def onward(side, t):
        return t < me_seq if side else t > me_seq

    def stage(side, c):
        @pl.loop(0, n_seq)
        def _(turn):
            t = turn if side else n_seq - 1 - turn

            @pl.when(onward(side, t))
            def _():
                @pl.when(fed[side])
                def _():
                    hop(side, c, t).wait_recv()
                    summed = part[c, t] + flow[side, c, t].astype(jnp.float32)
                    flow[side, c, t] = summed.astype(jnp.bfloat16)

                @pl.when(jnp.logical_not(fed[side]))
                def _():
                    flow[side, c, t] = part[c, t].astype(jnp.bfloat16)

                hop(side, c, t).start()

    def send_own(c):
        for step in direct:
            dp_copy(c, step).start()

    def pass_on(c):
        for step in direct:
            dp_copy(c, step).wait_recv()
        if relay:
            @pl.when(lax.rem(c, 2) == 0)
            def _():
                relay_copy(c, 1, 2).start()

            @pl.when(lax.rem(c, 2) == 1)
            def _():
                relay_copy(c, 2, 1).start()

    def input_share(c):
        kind, where = place(c)
        gx_acc[...] += nt(d_ref[c], w_buf[kind, :, where])

    def weight_share(c):
        if relay:
            relay_copy(c, 1, 2).wait_recv()
        others = gath[c].reshape((n_dp - 1) * slab, width)
        product = jnp.dot(latt_ref[:, :slab], d_ref[c], preferred_element_type=jnp.float32)
        product += jnp.dot(latt_ref[:, slab:], others, preferred_element_type=jnp.float32)
        part[c] = product.reshape(n_seq, rows, width)

    own_do.wait()
    lanes = lax.broadcasted_iota(jnp.int32, (slab, 128), 1)
    stat[...] = jnp.zeros_like(stat)

    @pl.loop(0, heads)
    def _(h):
        queries = q_hat[1, :, at(h)]
        keys = k_hat[:, :, at(h)].reshape(3 * slab, HD)
        values = v_hat[:, :, at(h)].reshape(3 * slab, HD)
        expo = jnp.exp(nt(queries, keys) * scale) * mask[...]
        row_total = jnp.sum(expo, axis=-1, keepdims=True)
        probs = expo * (1.0 / row_total)
        out_ref[:, at(h)] = jnp.dot(
            probs.astype(jnp.bfloat16), values, preferred_element_type=jnp.float32
        ).astype(jnp.bfloat16)
        d_probs = nt(do_buf[1, :, at(h)], values)
        row_delta = jnp.sum(probs * d_probs, axis=-1, keepdims=True)
        d_scores = (probs * (d_probs - row_delta) * scale).astype(jnp.bfloat16)
        d_qhat = jnp.dot(d_scores, keys, preferred_element_type=jnp.float32)
        raw = q_raw[:, at(h)]
        put(h // group, h, norm_back(raw, inv_rms(raw), q_gain, d_qhat))
        rows = jnp.where(lanes == 2 * h, row_total, stat[...])
        stat[...] = jnp.where(lanes == 2 * h + 1, row_delta, rows)

        @pl.when(lax.rem(h, group) == group - 1)
        def _():
            send_own(h // group)

    stat_t[1] = jnp.transpose(stat[...])[: stat_t.shape[1]]

    @pl.when(below)
    def _():
        stat_copy(0).start()

    @pl.when(above)
    def _():
        stat_copy(1).start()

    own_cols = pl.ds(pl.multiple_of(me_dp * block, block), block)
    latt_ref[:, :slab] = jnp.transpose(lat_buf[1, :, own_cols])
    for step in range(1, n_dp):
        clip_copy(step).wait_recv()
        latt_ref[:, step * slab : (step + 1) * slab] = jnp.transpose(clip_buf[step - 1])

    @pl.when(above)
    def _():
        do_copy(0).wait_recv()
        stat_copy(0).wait_recv()

    @pl.when(below)
    def _():
        do_copy(1).wait_recv()
        stat_copy(1).wait_recv()

    gx_acc[...] = jnp.zeros_like(gx_acc)

    def reverse(h):
        keys = k_hat[1, :, at(h)]
        values = v_hat[1, :, at(h)]
        queries = q_hat[:, :, at(h)].reshape(3 * slab, HD)
        upstream = do_buf[:, :, at(h)].reshape(3 * slab, HD)
        total = jnp.concatenate([stat_t[s, pl.ds(2 * h, 1), :] for s in range(3)], axis=1)
        delta = jnp.concatenate([stat_t[s, pl.ds(2 * h + 1, 1), :] for s in range(3)], axis=1)
        probs = jnp.exp(nt(keys, queries) * scale) * mask_t[...] * (1.0 / total)
        late = parts + 2 * (h // group)
        put(late + 1, h, jnp.dot(probs.astype(jnp.bfloat16), upstream, preferred_element_type=jnp.float32))
        d_scores = (probs * (nt(values, upstream) - delta) * scale).astype(jnp.bfloat16)
        d_khat = jnp.dot(d_scores, queries, preferred_element_type=jnp.float32)
        raw = k_raw[:, at(h)]
        put(late, h, norm_back(raw, inv_rms(raw), k_gain, d_khat))

    share = gx_ref.shape[0]

    def h_copy(step):
        peer = head_peer(step)
        return remote(
            gx_acc.at[pl.ds(pl.multiple_of(peer * share, share), share)],
            gx_recv.at[step - 1], h_ss.at[step - 1], h_rs.at[step - 1], {"head": peer},
        )

    @pl.loop(0, chunks + n_seq - 1)
    def _(tick):
        @pl.when((tick > 0) & (tick <= chunks))
        def _():
            weight_share(tick - 1)

        for side in range(2):
            lag = n_seq - 1 - me_seq if side else me_seq
            c = tick - 1 - lag

            @pl.when((c >= 0) & (c < chunks))
            def _():
                stage(side, c)

        @pl.when(tick < parts)
        def _():
            @pl.loop(0, group)
            def _(h):
                reverse(tick * group + h)

        @pl.when(tick < chunks)
        def _():
            pass_on(tick)

            @pl.when(tick < chunks - parts)
            def _():
                send_own(tick + parts)

            input_share(tick)

        @pl.when(tick == chunks - 1)
        def _():
            for step in range(1, n_head):
                h_copy(step).start()


    for step in range(1, n_head):
        h_copy(step).wait()
    total = gx_acc[pl.ds(pl.multiple_of(me_head * share, share), share)]
    for step in range(1, n_head):
        total = total + gx_recv[step - 1]
    gx_ref[...] = total.astype(gx_ref.dtype)

    @pl.loop(0, chunks)
    def _(c):
        kind, where = place(c)
        gw_ref[kind, :, where] = part[c, me_seq]
        for side in range(2):
            @pl.when(fed[side])
            def _():
                hop(side, c, me_seq).wait_recv()
                gw_ref[kind, :, where] += flow[side, c, me_seq].astype(jnp.float32)

            @pl.loop(0, n_seq)
            def _(t):
                @pl.when(onward(side, t))
                def _():
                    hop(side, c, t).wait_send()

        for step in direct:
            dp_copy(c, step).wait_send()
        if relay:
            relay_copy(c, 1, 2).wait_send()

    def settle(slot, side):
        lat_copy(side).wait_send()
        do_copy(side).wait_send()
        stat_copy(side).wait_send()
        for step in range(1, n_head):
            pass_copy(slot, step).wait_send()

    @pl.when(below)
    def _():
        settle(0, 0)

    @pl.when(above)
    def _():
        settle(2, 1)

    for step in range(1, n_dp):
        clip_copy(step).wait_send()


def layer(slab_tokens, w_three, q_gain, k_gain, neighbours, upstream):
    n_dp, n_seq, n_head = (lax.axis_size(axis) for axis in ("dp", "seq", "head"))
    slab = slab_tokens.shape[0]
    three, model_width, head_width = w_three.shape
    heads = head_width // HD
    group = 3 if heads % 3 == 0 else 1
    width = group * HD
    chunks = three * heads // group
    block = model_width // n_dp
    rows = block // n_seq
    share = slab // n_head
    stat_rows = -(-2 * heads // 8) * 8
    vmem = pl.BlockSpec(memory_space=pltpu.VMEM)
    anywhere = pl.BlockSpec(memory_space=pl.ANY)
    dma = pltpu.SemaphoreType.DMA
    bf16, f32 = jnp.bfloat16, jnp.float32
    return pl.pallas_call(
        functools.partial(layer_kernel, n_dp, n_seq, n_head),
        out_shape=(
            jax.ShapeDtypeStruct((slab, head_width), bf16),
            jax.ShapeDtypeStruct((three, rows, head_width), f32),
            jax.ShapeDtypeStruct((share, model_width), bf16),
        ),
        in_specs=[anywhere, anywhere, vmem, vmem, vmem, anywhere],
        out_specs=(vmem, vmem, vmem),
        scratch_shapes=[
            pltpu.VMEM((chunks, slab, width), bf16),
            pltpu.VMEM((block, n_dp * slab), bf16),
            pltpu.VMEM((chunks, n_dp - 1, slab, width), bf16),
            pltpu.VMEM((chunks, n_seq, rows, width), f32),
            pltpu.VMEM((2, chunks, n_seq, rows, width), bf16),
            pltpu.VMEM((slab, model_width), f32),
            pltpu.VMEM((n_head - 1, share, model_width), f32),
            pltpu.VMEM((3, slab, model_width), bf16),
            pltpu.VMEM((three, model_width, head_width), bf16),
            pltpu.VMEM((3, slab, head_width), bf16),
            pltpu.VMEM((slab, head_width), f32),
            pltpu.VMEM((slab, head_width), f32),
            pltpu.VMEM((3, slab, head_width), bf16),
            pltpu.VMEM((3, slab, head_width), bf16),
            pltpu.VMEM((3, slab, head_width), bf16),
            pltpu.VMEM((slab, 3 * slab), f32),
            pltpu.VMEM((slab, 3 * slab), f32),
            pltpu.VMEM((slab, 128), f32),
            pltpu.VMEM((3, stat_rows, slab), f32),
            pltpu.VMEM((n_dp - 1, slab, block), bf16),
            dma((2,)),
            dma((chunks,)),
            dma((2,)),
            dma((2,)),
            dma((2, n_head - 1)),
            dma((2, n_head - 1)),
            dma((2,)),
            dma((2,)),
            dma((2,)),
            dma((2,)),
            dma((n_dp - 1,)),
            dma((n_dp - 1,)),
            dma((chunks, n_dp - 1)),
            dma((chunks, n_dp - 1)),
            dma((2, chunks, n_seq)),
            dma((2, chunks, n_seq)),
            dma((n_head - 1,)),
            dma((n_head - 1,)),
        ],
        compiler_params=pltpu.CompilerParams(
            collective_id=0, has_side_effects=True, vmem_limit_bytes=60 * 1024 * 1024
        ),
        name="layer",
    )(slab_tokens, w_three, q_gain.reshape(1, HD), k_gain.reshape(1, HD), neighbours, upstream)


def local(latents, w_qkv, q_gain, k_gain, neighbours, grad_out):
    w_three = jnp.transpose(w_qkv, (1, 0, 2))
    attn_out, grad_w, grad_x = layer(
        latents[0], w_three, q_gain, k_gain, neighbours, grad_out[0]
    )
    return (attn_out[None], grad_x[None], jnp.transpose(grad_w, (1, 0, 2)))


def solution(mesh):
    in_specs = (P("dp", "seq", None), P(None, None, "head"), P(), P(), P(), P("dp", "seq", "head"))
    out_specs = (
        P("dp", "seq", "head"),
        P("dp", ("seq", "head"), None),
        P(("dp", "seq"), None, "head"),
    )
    return jax.shard_map(local, mesh=mesh, in_specs=in_specs, out_specs=out_specs, check_vma=False)
```

```python
import functools
import math

import jax
import jax.numpy as jnp
from jax import lax
from jax.experimental import pallas as pl
from jax.experimental.pallas import tpu as pltpu
from jax.sharding import PartitionSpec as P

MESH = pl.DeviceIdType.MESH

HD = 128
TILE = 64


EPS = 1e-06


def inv_rms(values):
    return lax.rsqrt(jnp.mean(values * values, axis=-1, keepdims=True) + EPS)


def norm_back(raw, inverse, gain, upstream):
    normed = raw * inverse
    weighted = upstream * gain
    return inverse * (weighted - normed * jnp.mean(weighted * normed, axis=-1, keepdims=True))


def remote(src, dst, send_sem, recv_sem, peer):
    return pltpu.make_async_remote_copy(
        src_ref=src,
        dst_ref=dst,
        send_sem=send_sem,
        recv_sem=recv_sem,
        device_id=peer,
        device_id_type=MESH,
    )


def layer_kernel(
    n_dp, n_seq, n_head, lat_ref, w_ref, qg_ref, kg_ref, near_ref, do_ref,
    out_ref, gw_ref, gx_ref,
    d_ref, latt_ref, gath, part, flow, gx_acc, gx_recv, lat_buf, w_buf, do_buf, q_raw, k_raw, q_hat, k_hat, v_hat, mask, mask_t, stat, stat_t, clip_buf,
    l_sem, w_sem, a_ss, a_rs, f_ss, f_rs, o_ss, o_rs, s_ss, s_rs, c_ss, c_rs,
    d_ss, d_rs, z_ss, z_rs, h_ss, h_rs,
):
    three, model_width, head_width = w_ref.shape
    slab = lat_ref.shape[0]
    chunks, _, width = d_ref.shape
    parts = chunks // three
    group = width // HD
    heads = head_width // HD
    half = slab // n_head
    block = model_width // n_dp
    scale = 1.0 / math.sqrt(HD)
    me_dp = lax.axis_index("dp")
    me_seq = lax.axis_index("seq")
    me_head = lax.axis_index("head")
    below = me_seq > 0
    above = me_seq < n_seq - 1

    def dp_peer(step, sign=1):
        if n_dp == 4:
            low, high = lax.rem(me_dp, 2), me_dp // 2
            if step % 2:
                low = 1 - low
            if step // 2:
                high = 1 - high
            return high * 2 + low
        return lax.rem(me_dp + n_dp + sign * step, n_dp)

    def head_peer(step, sign=1):
        return lax.rem(me_head + n_head + sign * step, n_head)

    own_lat = pltpu.make_async_copy(lat_ref, lat_buf.at[1], l_sem.at[0])
    own_do = pltpu.make_async_copy(do_ref, do_buf.at[1], l_sem.at[1])

    def cols(p):
        return pl.ds(pl.multiple_of(p * width, width), width)

    def w_copy(c):
        at = cols(lax.rem(c, parts))
        return pltpu.make_async_copy(
            w_ref.at[c // parts, :, at], w_buf.at[c // parts, :, at], w_sem.at[c]
        )

    own_lat.start()

    @pl.loop(0, chunks)
    def _(c):
        w_copy(c).start()

    own_do.start()

    barrier = pltpu.get_barrier_semaphore()

    @pl.when(below)
    def _():
        pl.semaphore_signal(barrier, inc=1, device_id={"seq": me_seq - 1}, device_id_type=MESH)

    @pl.when(above)
    def _():
        pl.semaphore_signal(barrier, inc=1, device_id={"seq": me_seq + 1}, device_id_type=MESH)

    for step in range(1, n_dp):
        pl.semaphore_signal(
            barrier, inc=1, device_id={"dp": dp_peer(step, -1)}, device_id_type=MESH
        )
    for step in range(1, n_head):
        pl.semaphore_signal(
            barrier, inc=1, device_id={"head": head_peer(step, -1)}, device_id_type=MESH
        )
    sides = jnp.minimum(me_seq, 1) + jnp.minimum(n_seq - 1 - me_seq, 1)
    pl.semaphore_wait(barrier, n_dp - 1 + n_head - 1 + sides)

    my_rows = pl.ds(pl.multiple_of(me_head * half, half), half)

    def lat_copy(side):
        return remote(
            lat_ref.at[my_rows], lat_buf.at[2 - 2 * side, my_rows],
            a_ss.at[side], a_rs.at[side], {"seq": me_seq + 2 * side - 1},
        )

    def do_copy(side):
        return remote(
            do_ref, do_buf.at[2 - 2 * side],
            o_ss.at[side], o_rs.at[side], {"seq": me_seq + 2 * side - 1},
        )

    def stat_copy(side):
        return remote(
            stat_t.at[1], stat_t.at[2 - 2 * side],
            s_ss.at[side], s_rs.at[side], {"seq": me_seq + 2 * side - 1},
        )

    def pass_copy(slot, step):
        return remote(
            lat_buf.at[slot, my_rows], lat_buf.at[slot, my_rows],
            f_ss.at[slot // 2, step - 1], f_rs.at[slot // 2, step - 1],
            {"head": head_peer(step)},
        )

    def clip_copy(step):
        peer = dp_peer(step)
        return remote(
            lat_ref.at[:, pl.ds(pl.multiple_of(peer * block, block), block)],
            clip_buf.at[step - 1], c_ss.at[step - 1], c_rs.at[step - 1], {"dp": peer},
        )

    @pl.when(below)
    def _():
        lat_copy(0).start()

    @pl.when(above)
    def _():
        lat_copy(1).start()

    for step in range(1, n_dp):
        clip_copy(step).start()

    @pl.when(below)
    def _():
        do_copy(0).start()

    @pl.when(above)
    def _():
        do_copy(1).start()

    def clear(slot):
        lat_buf[slot] = jnp.zeros_like(lat_buf[slot])
        do_buf[slot] = jnp.zeros_like(do_buf[slot])
        stat_t[slot] = jnp.ones_like(stat_t[slot])

    @pl.when(me_seq == 0)
    def _():
        clear(0)

    @pl.when(me_seq == n_seq - 1)
    def _():
        clear(2)

    tiles = near_ref.shape[0]
    near = near_ref[...]
    tile_ids = lax.broadcasted_iota(jnp.int32, (tiles, tiles), 1)
    hits = jnp.zeros((tiles, tiles), jnp.float32)
    for slot in range(near_ref.shape[1]):
        hits = jnp.where(near[:, slot : slot + 1] == tile_ids, 1.0, hits)
    hits = hits.astype(jnp.bfloat16)
    own_tile = me_seq * (slab // TILE)
    first_tile = own_tile - slab // TILE
    own_pick = lax.broadcasted_iota(jnp.int32, (slab, tiles), 1) == (
        lax.broadcasted_iota(jnp.int32, (slab, tiles), 0) // TILE + own_tile
    )
    own_pick = jnp.where(own_pick, 1.0, 0.0).astype(jnp.bfloat16)
    wide_pick = lax.broadcasted_iota(jnp.int32, (tiles, 3 * slab), 0) == (
        lax.broadcasted_iota(jnp.int32, (tiles, 3 * slab), 1) // TILE + first_tile
    )
    wide_pick = jnp.where(wide_pick, 1.0, 0.0).astype(jnp.bfloat16)
    picked = jnp.dot(own_pick, hits, preferred_element_type=jnp.float32).astype(jnp.bfloat16)
    mask[...] = jnp.dot(picked, wide_pick, preferred_element_type=jnp.float32)
    picked = lax.dot_general(
        own_pick, hits, (((1,), (1,)), ((), ())), preferred_element_type=jnp.float32
    ).astype(jnp.bfloat16)
    mask_t[...] = jnp.dot(picked, wide_pick, preferred_element_type=jnp.float32)

    q_gain = qg_ref[...]
    k_gain = kg_ref[...]
    own_lat.wait()

    def arrive(slot, side):
        lat_copy(side).wait_recv()
        for step in range(1, n_head):
            pass_copy(slot, step).start()

    def passed(slot):
        for step in range(1, n_head):
            pass_copy(slot, step).wait_recv()

    @pl.loop(0, 3)
    def _(turn):
        slot = lax.rem(turn + 1, 3)

        @pl.when(turn == 1)
        def _():
            @pl.when(above)
            def _():
                arrive(2, 0)

            @pl.when(below)
            def _():
                arrive(0, 1)

            @pl.when(above)
            def _():
                passed(2)

        @pl.when((turn == 2) & below)
        def _():
            passed(0)

        for kind in range(three):
            @pl.loop(0, parts)
            def _(p):
                @pl.when(turn == 0)
                def _():
                    w_copy(kind * parts + p).wait()

                raw = jnp.dot(
                    lat_buf[slot], w_buf[kind, :, cols(p)], preferred_element_type=jnp.float32
                )
                if kind == 2:
                    v_hat[slot, :, cols(p)] = raw.astype(jnp.bfloat16)
                else:
                    kept, normed, gain = ((q_raw, q_hat, q_gain), (k_raw, k_hat, k_gain))[kind]

                    @pl.when(turn == 0)
                    def _():
                        kept[:, cols(p)] = raw

                    pieces = []
                    for h in range(group):
                        piece = raw[:, h * HD : (h + 1) * HD]
                        pieces.append((piece * inv_rms(piece) * gain).astype(jnp.bfloat16))
                    normed[slot, :, cols(p)] = jnp.concatenate(pieces, axis=1)

    def at(h):
        return pl.ds(pl.multiple_of(h * HD, HD), HD)

    def nt(a, b):
        return lax.dot_general(a, b, (((1,), (1,)), ((), ())), preferred_element_type=jnp.float32)

    def put(position, h, value):
        d_ref[position, :, at(lax.rem(h, group))] = value.astype(jnp.bfloat16)

    def place(position):
        late = jnp.maximum(position - parts, 0)
        is_late = jnp.where(position >= parts, 1, 0)
        kind = is_late * (1 + lax.rem(late, 2))
        p = is_late * (late // 2) + (1 - is_late) * position
        return kind, cols(p)

    relay = n_dp == 4
    direct = (1, 2) if relay else tuple(range(1, n_dp))
    rows = gw_ref.shape[1]

    def dp_copy(c, step):
        return remote(
            d_ref.at[c], gath.at[c, step - 1],
            d_ss.at[c, step - 1], d_rs.at[c, step - 1], {"dp": dp_peer(step)},
        )

    def relay_copy(c, via, onward):
        return remote(
            gath.at[c, via - 1], gath.at[c, 2],
            d_ss.at[c, 2], d_rs.at[c, 2], {"dp": dp_peer(onward)},
        )

    def hop(side, c, t):
        peer = lax.rem(me_seq + n_seq + 1 - 2 * side, n_seq)
        return remote(
            flow.at[side, c, t], flow.at[side, c, t],
            z_ss.at[side, c, t], z_rs.at[side, c, t], {"seq": peer},
        )

    fed = (below, above)

    def onward(side, t):
        return t < me_seq if side else t > me_seq

    def stage(side, c):
        @pl.loop(0, n_seq)
        def _(turn):
            t = turn if side else n_seq - 1 - turn

            @pl.when(onward(side, t))
            def _():
                @pl.when(fed[side])
                def _():
                    hop(side, c, t).wait_recv()
                    summed = part[c, t] + flow[side, c, t].astype(jnp.float32)
                    flow[side, c, t] = summed.astype(jnp.bfloat16)

                @pl.when(jnp.logical_not(fed[side]))
                def _():
                    flow[side, c, t] = part[c, t].astype(jnp.bfloat16)

                hop(side, c, t).start()

    def send_own(c):
        for step in direct:
            dp_copy(c, step).start()

    def pass_on(c):
        for step in direct:
            dp_copy(c, step).wait_recv()
        if relay:
            @pl.when(lax.rem(c, 2) == 0)
            def _():
                relay_copy(c, 1, 2).start()

            @pl.when(lax.rem(c, 2) == 1)
            def _():
                relay_copy(c, 2, 1).start()

    def input_share(c):
        kind, where = place(c)
        gx_acc[...] += nt(d_ref[c], w_buf[kind, :, where])

    def weight_share(c):
        if relay:
            relay_copy(c, 1, 2).wait_recv()
        others = gath[c].reshape((n_dp - 1) * slab, width)
        product = jnp.dot(latt_ref[:, :slab], d_ref[c], preferred_element_type=jnp.float32)
        product += jnp.dot(latt_ref[:, slab:], others, preferred_element_type=jnp.float32)
        part[c] = product.reshape(n_seq, rows, width)

    own_do.wait()
    lanes = lax.broadcasted_iota(jnp.int32, (slab, 128), 1)
    stat[...] = jnp.zeros_like(stat)

    @pl.loop(0, heads)
    def _(h):
        queries = q_hat[1, :, at(h)]
        keys = k_hat[:, :, at(h)].reshape(3 * slab, HD)
        values = v_hat[:, :, at(h)].reshape(3 * slab, HD)
        expo = jnp.exp(nt(queries, keys) * scale) * mask[...]
        row_total = jnp.sum(expo, axis=-1, keepdims=True)
        probs = expo * (1.0 / row_total)
        out_ref[:, at(h)] = jnp.dot(
            probs.astype(jnp.bfloat16), values, preferred_element_type=jnp.float32
        ).astype(jnp.bfloat16)
        d_probs = nt(do_buf[1, :, at(h)], values)
        row_delta = jnp.sum(probs * d_probs, axis=-1, keepdims=True)
        d_scores = (probs * (d_probs - row_delta) * scale).astype(jnp.bfloat16)
        d_qhat = jnp.dot(d_scores, keys, preferred_element_type=jnp.float32)
        raw = q_raw[:, at(h)]
        put(h // group, h, norm_back(raw, inv_rms(raw), q_gain, d_qhat))
        rows = jnp.where(lanes == 2 * h, row_total, stat[...])
        stat[...] = jnp.where(lanes == 2 * h + 1, row_delta, rows)

        @pl.when(lax.rem(h, group) == group - 1)
        def _():
            send_own(h // group)

    stat_t[1] = jnp.transpose(stat[...])[: stat_t.shape[1]]

    @pl.when(below)
    def _():
        stat_copy(0).start()

    @pl.when(above)
    def _():
        stat_copy(1).start()

    own_cols = pl.ds(pl.multiple_of(me_dp * block, block), block)
    latt_ref[:, :slab] = jnp.transpose(lat_buf[1, :, own_cols])
    for step in range(1, n_dp):
        clip_copy(step).wait_recv()
        latt_ref[:, step * slab : (step + 1) * slab] = jnp.transpose(clip_buf[step - 1])

    gx_acc[...] = jnp.zeros_like(gx_acc)

    def reverse(h):
        keys = k_hat[1, :, at(h)]
        values = v_hat[1, :, at(h)]
        queries = q_hat[:, :, at(h)].reshape(3 * slab, HD)
        upstream = do_buf[:, :, at(h)].reshape(3 * slab, HD)
        total = jnp.concatenate([stat_t[s, pl.ds(2 * h, 1), :] for s in range(3)], axis=1)
        delta = jnp.concatenate([stat_t[s, pl.ds(2 * h + 1, 1), :] for s in range(3)], axis=1)
        probs = jnp.exp(nt(keys, queries) * scale) * mask_t[...] * (1.0 / total)
        late = parts + 2 * (h // group)
        put(late + 1, h, jnp.dot(probs.astype(jnp.bfloat16), upstream, preferred_element_type=jnp.float32))
        d_scores = (probs * (nt(values, upstream) - delta) * scale).astype(jnp.bfloat16)
        d_khat = jnp.dot(d_scores, queries, preferred_element_type=jnp.float32)
        raw = k_raw[:, at(h)]
        put(late, h, norm_back(raw, inv_rms(raw), k_gain, d_khat))

    share = gx_ref.shape[0]

    def h_copy(step):
        peer = head_peer(step)
        return remote(
            gx_acc.at[pl.ds(pl.multiple_of(peer * share, share), share)],
            gx_recv.at[step - 1], h_ss.at[step - 1], h_rs.at[step - 1], {"head": peer},
        )

    @pl.loop(0, chunks + n_seq - 1)
    def _(tick):
        @pl.when(tick < chunks)
        def _():
            pass_on(tick)

        @pl.when((tick >= parts) & (tick < chunks - parts))
        def _():
            send_own(tick + parts)

        @pl.when((tick > 0) & (tick <= chunks))
        def _():
            weight_share(tick - 1)

        for side in range(2):
            lag = n_seq - 1 - me_seq if side else me_seq
            c = tick - 1 - lag

            @pl.when((c >= 0) & (c < chunks))
            def _():
                stage(side, c)

        @pl.when((tick == 0) & above)
        def _():
            do_copy(0).wait_recv()
            stat_copy(0).wait_recv()

        @pl.when((tick == 0) & below)
        def _():
            do_copy(1).wait_recv()
            stat_copy(1).wait_recv()

        @pl.when(tick < parts)
        def _():
            @pl.loop(0, group)
            def _(h):
                reverse(tick * group + h)

            send_own(tick + parts)

        @pl.when(tick < chunks)
        def _():
            input_share(tick)

        @pl.when(tick == chunks - 1)
        def _():
            for step in range(1, n_head):
                h_copy(step).start()


    for step in range(1, n_head):
        h_copy(step).wait()
    total = gx_acc[pl.ds(pl.multiple_of(me_head * share, share), share)]
    for step in range(1, n_head):
        total = total + gx_recv[step - 1]
    gx_ref[...] = total.astype(gx_ref.dtype)

    @pl.loop(0, chunks)
    def _(c):
        kind, where = place(c)
        gw_ref[kind, :, where] = part[c, me_seq]
        for side in range(2):
            @pl.when(fed[side])
            def _():
                hop(side, c, me_seq).wait_recv()
                gw_ref[kind, :, where] += flow[side, c, me_seq].astype(jnp.float32)

            @pl.loop(0, n_seq)
            def _(t):
                @pl.when(onward(side, t))
                def _():
                    hop(side, c, t).wait_send()

        for step in direct:
            dp_copy(c, step).wait_send()
        if relay:
            relay_copy(c, 1, 2).wait_send()

    def settle(slot, side):
        lat_copy(side).wait_send()
        do_copy(side).wait_send()
        stat_copy(side).wait_send()
        for step in range(1, n_head):
            pass_copy(slot, step).wait_send()

    @pl.when(below)
    def _():
        settle(0, 0)

    @pl.when(above)
    def _():
        settle(2, 1)

    for step in range(1, n_dp):
        clip_copy(step).wait_send()


def layer(slab_tokens, w_three, q_gain, k_gain, neighbours, upstream):
    n_dp, n_seq, n_head = (lax.axis_size(axis) for axis in ("dp", "seq", "head"))
    slab = slab_tokens.shape[0]
    three, model_width, head_width = w_three.shape
    heads = head_width // HD
    group = 3 if heads % 3 == 0 else 1
    width = group * HD
    chunks = three * heads // group
    block = model_width // n_dp
    rows = block // n_seq
    share = slab // n_head
    stat_rows = -(-2 * heads // 8) * 8
    vmem = pl.BlockSpec(memory_space=pltpu.VMEM)
    anywhere = pl.BlockSpec(memory_space=pl.ANY)
    dma = pltpu.SemaphoreType.DMA
    bf16, f32 = jnp.bfloat16, jnp.float32
    return pl.pallas_call(
        functools.partial(layer_kernel, n_dp, n_seq, n_head),
        out_shape=(
            jax.ShapeDtypeStruct((slab, head_width), bf16),
            jax.ShapeDtypeStruct((three, rows, head_width), f32),
            jax.ShapeDtypeStruct((share, model_width), bf16),
        ),
        in_specs=[anywhere, anywhere, vmem, vmem, vmem, anywhere],
        out_specs=(vmem, vmem, vmem),
        scratch_shapes=[
            pltpu.VMEM((chunks, slab, width), bf16),
            pltpu.VMEM((block, n_dp * slab), bf16),
            pltpu.VMEM((chunks, n_dp - 1, slab, width), bf16),
            pltpu.VMEM((chunks, n_seq, rows, width), f32),
            pltpu.VMEM((2, chunks, n_seq, rows, width), bf16),
            pltpu.VMEM((slab, model_width), f32),
            pltpu.VMEM((n_head - 1, share, model_width), f32),
            pltpu.VMEM((3, slab, model_width), bf16),
            pltpu.VMEM((three, model_width, head_width), bf16),
            pltpu.VMEM((3, slab, head_width), bf16),
            pltpu.VMEM((slab, head_width), f32),
            pltpu.VMEM((slab, head_width), f32),
            pltpu.VMEM((3, slab, head_width), bf16),
            pltpu.VMEM((3, slab, head_width), bf16),
            pltpu.VMEM((3, slab, head_width), bf16),
            pltpu.VMEM((slab, 3 * slab), f32),
            pltpu.VMEM((slab, 3 * slab), f32),
            pltpu.VMEM((slab, 128), f32),
            pltpu.VMEM((3, stat_rows, slab), f32),
            pltpu.VMEM((n_dp - 1, slab, block), bf16),
            dma((2,)),
            dma((chunks,)),
            dma((2,)),
            dma((2,)),
            dma((2, n_head - 1)),
            dma((2, n_head - 1)),
            dma((2,)),
            dma((2,)),
            dma((2,)),
            dma((2,)),
            dma((n_dp - 1,)),
            dma((n_dp - 1,)),
            dma((chunks, n_dp - 1)),
            dma((chunks, n_dp - 1)),
            dma((2, chunks, n_seq)),
            dma((2, chunks, n_seq)),
            dma((n_head - 1,)),
            dma((n_head - 1,)),
        ],
        compiler_params=pltpu.CompilerParams(
            collective_id=0, has_side_effects=True, vmem_limit_bytes=60 * 1024 * 1024
        ),
        name="layer",
    )(slab_tokens, w_three, q_gain.reshape(1, HD), k_gain.reshape(1, HD), neighbours, upstream)


def local(latents, w_qkv, q_gain, k_gain, neighbours, grad_out):
    w_three = jnp.transpose(w_qkv, (1, 0, 2))
    attn_out, grad_w, grad_x = layer(
        latents[0], w_three, q_gain, k_gain, neighbours, grad_out[0]
    )
    return (attn_out[None], grad_x[None], jnp.transpose(grad_w, (1, 0, 2)))


def solution(mesh):
    in_specs = (P("dp", "seq", None), P(None, None, "head"), P(), P(), P(), P("dp", "seq", "head"))
    out_specs = (
        P("dp", "seq", "head"),
        P("dp", ("seq", "head"), None),
        P(("dp", "seq"), None, "head"),
    )
    return jax.shard_map(local, mesh=mesh, in_specs=in_specs, out_specs=out_specs, check_vma=False)
```

```python
import functools
import math

import jax
import jax.numpy as jnp
from jax import lax
from jax.experimental import pallas as pl
from jax.experimental.pallas import tpu as pltpu
from jax.sharding import PartitionSpec as P

MESH = pl.DeviceIdType.MESH

HD = 128
TILE = 64


EPS = 1e-06


def inv_rms(values):
    return lax.rsqrt(jnp.mean(values * values, axis=-1, keepdims=True) + EPS)


def norm_back(raw, inverse, gain, upstream):
    normed = raw * inverse
    weighted = upstream * gain
    return inverse * (weighted - normed * jnp.mean(weighted * normed, axis=-1, keepdims=True))


def remote(src, dst, send_sem, recv_sem, peer):
    return pltpu.make_async_remote_copy(
        src_ref=src,
        dst_ref=dst,
        send_sem=send_sem,
        recv_sem=recv_sem,
        device_id=peer,
        device_id_type=MESH,
    )


def layer_kernel(
    n_dp, n_seq, n_head, lat_ref, w_ref, qg_ref, kg_ref, near_ref, do_ref,
    out_ref, gw_ref, gx_ref,
    d_ref, latt_ref, gath, part, flow, gx_acc, gx_recv, lat_buf, w_buf, do_buf, q_raw, k_raw, q_hat, k_hat, v_hat, mask, mask_t, stat, stat_t, clip_buf,
    l_sem, w_sem, a_ss, a_rs, f_ss, f_rs, o_ss, o_rs, s_ss, s_rs, c_ss, c_rs,
    d_ss, d_rs, z_ss, z_rs, h_ss, h_rs,
):
    three, model_width, head_width = w_ref.shape
    slab = lat_ref.shape[0]
    chunks, _, width = d_ref.shape
    parts = chunks // three
    group = width // HD
    heads = head_width // HD
    half = slab // n_head
    block = model_width // n_dp
    scale = 1.0 / math.sqrt(HD)
    me_dp = lax.axis_index("dp")
    me_seq = lax.axis_index("seq")
    me_head = lax.axis_index("head")
    below = me_seq > 0
    above = me_seq < n_seq - 1

    def dp_peer(step, sign=1):
        if n_dp == 4:
            low, high = lax.rem(me_dp, 2), me_dp // 2
            if step % 2:
                low = 1 - low
            if step // 2:
                high = 1 - high
            return high * 2 + low
        return lax.rem(me_dp + n_dp + sign * step, n_dp)

    def head_peer(step, sign=1):
        return lax.rem(me_head + n_head + sign * step, n_head)

    own_lat = pltpu.make_async_copy(lat_ref, lat_buf.at[1], l_sem.at[0])
    own_do = pltpu.make_async_copy(do_ref, do_buf.at[1], l_sem.at[1])

    def cols(p):
        return pl.ds(pl.multiple_of(p * width, width), width)

    def w_copy(c):
        at = cols(lax.rem(c, parts))
        return pltpu.make_async_copy(
            w_ref.at[c // parts, :, at], w_buf.at[c // parts, :, at], w_sem.at[c]
        )

    own_lat.start()

    @pl.loop(0, chunks)
    def _(c):
        w_copy(c).start()

    own_do.start()

    barrier = pltpu.get_barrier_semaphore()

    @pl.when(below)
    def _():
        pl.semaphore_signal(barrier, inc=1, device_id={"seq": me_seq - 1}, device_id_type=MESH)

    @pl.when(above)
    def _():
        pl.semaphore_signal(barrier, inc=1, device_id={"seq": me_seq + 1}, device_id_type=MESH)

    for step in range(1, n_dp):
        pl.semaphore_signal(
            barrier, inc=1, device_id={"dp": dp_peer(step, -1)}, device_id_type=MESH
        )
    for step in range(1, n_head):
        pl.semaphore_signal(
            barrier, inc=1, device_id={"head": head_peer(step, -1)}, device_id_type=MESH
        )
    sides = jnp.minimum(me_seq, 1) + jnp.minimum(n_seq - 1 - me_seq, 1)
    pl.semaphore_wait(barrier, n_dp - 1 + n_head - 1 + sides)

    my_rows = pl.ds(pl.multiple_of(me_head * half, half), half)

    def lat_copy(side):
        return remote(
            lat_ref.at[my_rows], lat_buf.at[2 - 2 * side, my_rows],
            a_ss.at[side], a_rs.at[side], {"seq": me_seq + 2 * side - 1},
        )

    def do_copy(side):
        return remote(
            do_ref, do_buf.at[2 - 2 * side],
            o_ss.at[side], o_rs.at[side], {"seq": me_seq + 2 * side - 1},
        )

    def stat_copy(side):
        return remote(
            stat_t.at[1], stat_t.at[2 - 2 * side],
            s_ss.at[side], s_rs.at[side], {"seq": me_seq + 2 * side - 1},
        )

    def pass_copy(slot, step):
        return remote(
            lat_buf.at[slot, my_rows], lat_buf.at[slot, my_rows],
            f_ss.at[slot // 2, step - 1], f_rs.at[slot // 2, step - 1],
            {"head": head_peer(step)},
        )

    def clip_copy(step):
        peer = dp_peer(step)
        return remote(
            lat_ref.at[:, pl.ds(pl.multiple_of(peer * block, block), block)],
            clip_buf.at[step - 1], c_ss.at[step - 1], c_rs.at[step - 1], {"dp": peer},
        )

    @pl.when(below)
    def _():
        lat_copy(0).start()

    @pl.when(above)
    def _():
        lat_copy(1).start()

    for step in range(1, n_dp):
        clip_copy(step).start()

    @pl.when(below)
    def _():
        do_copy(0).start()

    @pl.when(above)
    def _():
        do_copy(1).start()

    def clear(slot):
        lat_buf[slot] = jnp.zeros_like(lat_buf[slot])
        do_buf[slot] = jnp.zeros_like(do_buf[slot])
        stat_t[slot] = jnp.ones_like(stat_t[slot])

    @pl.when(me_seq == 0)
    def _():
        clear(0)

    @pl.when(me_seq == n_seq - 1)
    def _():
        clear(2)

    tiles = near_ref.shape[0]
    near = near_ref[...]
    tile_ids = lax.broadcasted_iota(jnp.int32, (tiles, tiles), 1)
    hits = jnp.zeros((tiles, tiles), jnp.float32)
    for slot in range(near_ref.shape[1]):
        hits = jnp.where(near[:, slot : slot + 1] == tile_ids, 1.0, hits)
    hits = hits.astype(jnp.bfloat16)
    own_tile = me_seq * (slab // TILE)
    first_tile = own_tile - slab // TILE
    own_pick = lax.broadcasted_iota(jnp.int32, (slab, tiles), 1) == (
        lax.broadcasted_iota(jnp.int32, (slab, tiles), 0) // TILE + own_tile
    )
    own_pick = jnp.where(own_pick, 1.0, 0.0).astype(jnp.bfloat16)
    wide_pick = lax.broadcasted_iota(jnp.int32, (tiles, 3 * slab), 0) == (
        lax.broadcasted_iota(jnp.int32, (tiles, 3 * slab), 1) // TILE + first_tile
    )
    wide_pick = jnp.where(wide_pick, 1.0, 0.0).astype(jnp.bfloat16)
    picked = jnp.dot(own_pick, hits, preferred_element_type=jnp.float32).astype(jnp.bfloat16)
    mask[...] = jnp.dot(picked, wide_pick, preferred_element_type=jnp.float32)
    picked = lax.dot_general(
        own_pick, hits, (((1,), (1,)), ((), ())), preferred_element_type=jnp.float32
    ).astype(jnp.bfloat16)
    mask_t[...] = jnp.dot(picked, wide_pick, preferred_element_type=jnp.float32)

    q_gain = qg_ref[...]
    k_gain = kg_ref[...]
    own_lat.wait()

    def arrive(slot, side):
        lat_copy(side).wait_recv()
        for step in range(1, n_head):
            pass_copy(slot, step).start()

    def passed(slot):
        for step in range(1, n_head):
            pass_copy(slot, step).wait_recv()

    @pl.loop(0, 3)
    def _(turn):
        slot = lax.rem(turn + 1, 3)

        @pl.when(turn == 1)
        def _():
            @pl.when(above)
            def _():
                arrive(2, 0)

            @pl.when(below)
            def _():
                arrive(0, 1)

            @pl.when(above)
            def _():
                passed(2)

        @pl.when((turn == 2) & below)
        def _():
            passed(0)

        for kind in range(three):
            @pl.loop(0, parts)
            def _(p):
                @pl.when(turn == 0)
                def _():
                    w_copy(kind * parts + p).wait()

                raw = jnp.dot(
                    lat_buf[slot], w_buf[kind, :, cols(p)], preferred_element_type=jnp.float32
                )
                if kind == 2:
                    v_hat[slot, :, cols(p)] = raw.astype(jnp.bfloat16)
                else:
                    kept, normed, gain = ((q_raw, q_hat, q_gain), (k_raw, k_hat, k_gain))[kind]

                    @pl.when(turn == 0)
                    def _():
                        kept[:, cols(p)] = raw

                    pieces = []
                    for h in range(group):
                        piece = raw[:, h * HD : (h + 1) * HD]
                        pieces.append((piece * inv_rms(piece) * gain).astype(jnp.bfloat16))
                    normed[slot, :, cols(p)] = jnp.concatenate(pieces, axis=1)

    def at(h):
        return pl.ds(pl.multiple_of(h * HD, HD), HD)

    def nt(a, b):
        return lax.dot_general(a, b, (((1,), (1,)), ((), ())), preferred_element_type=jnp.float32)

    def put(position, h, value):
        d_ref[position, :, at(lax.rem(h, group))] = value.astype(jnp.bfloat16)

    def place(position):
        late = jnp.maximum(position - parts, 0)
        is_late = jnp.where(position >= parts, 1, 0)
        kind = is_late * (1 + lax.rem(late, 2))
        p = is_late * (late // 2) + (1 - is_late) * position
        return kind, cols(p)

    relay = n_dp == 4
    direct = (1, 2) if relay else tuple(range(1, n_dp))
    rows = gw_ref.shape[1]

    def dp_copy(c, step):
        return remote(
            d_ref.at[c], gath.at[c, step - 1],
            d_ss.at[c, step - 1], d_rs.at[c, step - 1], {"dp": dp_peer(step)},
        )

    def relay_copy(c, via, onward):
        return remote(
            gath.at[c, via - 1], gath.at[c, 2],
            d_ss.at[c, 2], d_rs.at[c, 2], {"dp": dp_peer(onward)},
        )

    def hop(side, c, t):
        peer = lax.rem(me_seq + n_seq + 1 - 2 * side, n_seq)
        return remote(
            flow.at[side, c, t], flow.at[side, c, t],
            z_ss.at[side, c, t], z_rs.at[side, c, t], {"seq": peer},
        )

    fed = (below, above)

    def onward(side, t):
        return t < me_seq if side else t > me_seq

    def stage(side, c):
        @pl.loop(0, n_seq)
        def _(turn):
            t = turn if side else n_seq - 1 - turn

            @pl.when(onward(side, t))
            def _():
                @pl.when(fed[side])
                def _():
                    hop(side, c, t).wait_recv()
                    summed = part[c, t] + flow[side, c, t].astype(jnp.float32)
                    flow[side, c, t] = summed.astype(jnp.bfloat16)

                @pl.when(jnp.logical_not(fed[side]))
                def _():
                    flow[side, c, t] = part[c, t].astype(jnp.bfloat16)

                hop(side, c, t).start()

    def send_own(c):
        for step in direct:
            dp_copy(c, step).start()

    def pass_on(c):
        for step in direct:
            dp_copy(c, step).wait_recv()
        if relay:
            @pl.when(lax.rem(c, 2) == 0)
            def _():
                relay_copy(c, 1, 2).start()

            @pl.when(lax.rem(c, 2) == 1)
            def _():
                relay_copy(c, 2, 1).start()

    def input_share(c):
        kind, where = place(c)
        gx_acc[...] += nt(d_ref[c], w_buf[kind, :, where])

    def weight_share(c):
        if relay:
            relay_copy(c, 1, 2).wait_recv()
        others = gath[c].reshape((n_dp - 1) * slab, width)
        product = jnp.dot(latt_ref[:, :slab], d_ref[c], preferred_element_type=jnp.float32)
        product += jnp.dot(latt_ref[:, slab:], others, preferred_element_type=jnp.float32)
        part[c] = product.reshape(n_seq, rows, width)

    own_do.wait()
    lanes = lax.broadcasted_iota(jnp.int32, (slab, 128), 1)
    stat[...] = jnp.zeros_like(stat)

    @pl.loop(0, heads)
    def _(h):
        queries = q_hat[1, :, at(h)]
        keys = k_hat[:, :, at(h)].reshape(3 * slab, HD)
        values = v_hat[:, :, at(h)].reshape(3 * slab, HD)
        expo = jnp.exp(nt(queries, keys) * scale) * mask[...]
        row_total = jnp.sum(expo, axis=-1, keepdims=True)
        probs = expo * (1.0 / row_total)
        out_ref[:, at(h)] = jnp.dot(
            probs.astype(jnp.bfloat16), values, preferred_element_type=jnp.float32
        ).astype(jnp.bfloat16)
        d_probs = nt(do_buf[1, :, at(h)], values)
        row_delta = jnp.sum(probs * d_probs, axis=-1, keepdims=True)
        d_scores = (probs * (d_probs - row_delta) * scale).astype(jnp.bfloat16)
        d_qhat = jnp.dot(d_scores, keys, preferred_element_type=jnp.float32)
        raw = q_raw[:, at(h)]
        put(h // group, h, norm_back(raw, inv_rms(raw), q_gain, d_qhat))
        rows = jnp.where(lanes == 2 * h, row_total, stat[...])
        stat[...] = jnp.where(lanes == 2 * h + 1, row_delta, rows)

        @pl.when(lax.rem(h, group) == group - 1)
        def _():
            send_own(h // group)

    stat_t[1] = jnp.transpose(stat[...])[: stat_t.shape[1]]

    @pl.when(below)
    def _():
        stat_copy(0).start()

    @pl.when(above)
    def _():
        stat_copy(1).start()

    own_cols = pl.ds(pl.multiple_of(me_dp * block, block), block)
    latt_ref[:, :slab] = jnp.transpose(lat_buf[1, :, own_cols])
    for step in range(1, n_dp):
        clip_copy(step).wait_recv()
        latt_ref[:, step * slab : (step + 1) * slab] = jnp.transpose(clip_buf[step - 1])

    gx_acc[...] = jnp.zeros_like(gx_acc)

    def reverse(h):
        keys = k_hat[1, :, at(h)]
        values = v_hat[1, :, at(h)]
        queries = q_hat[:, :, at(h)].reshape(3 * slab, HD)
        upstream = do_buf[:, :, at(h)].reshape(3 * slab, HD)
        total = jnp.concatenate([stat_t[s, pl.ds(2 * h, 1), :] for s in range(3)], axis=1)
        delta = jnp.concatenate([stat_t[s, pl.ds(2 * h + 1, 1), :] for s in range(3)], axis=1)
        probs = jnp.exp(nt(keys, queries) * scale) * mask_t[...] * (1.0 / total)
        late = parts + 2 * (h // group)
        put(late + 1, h, jnp.dot(probs.astype(jnp.bfloat16), upstream, preferred_element_type=jnp.float32))
        d_scores = (probs * (nt(values, upstream) - delta) * scale).astype(jnp.bfloat16)
        d_khat = jnp.dot(d_scores, queries, preferred_element_type=jnp.float32)
        raw = k_raw[:, at(h)]
        put(late, h, norm_back(raw, inv_rms(raw), k_gain, d_khat))

    share = gx_ref.shape[0]

    def h_copy(step):
        peer = head_peer(step)
        return remote(
            gx_acc.at[pl.ds(pl.multiple_of(peer * share, share), share)],
            gx_recv.at[step - 1], h_ss.at[step - 1], h_rs.at[step - 1], {"head": peer},
        )

    @pl.loop(0, chunks + n_seq - 1)
    def _(tick):
        @pl.when(tick < chunks)
        def _():
            pass_on(tick)

        @pl.when((tick > 0) & (tick < chunks - parts))
        def _():
            send_own(tick + parts)

        @pl.when((tick > 0) & (tick <= chunks))
        def _():
            weight_share(tick - 1)

        for side in range(2):
            lag = n_seq - 1 - me_seq if side else me_seq
            c = tick - 1 - lag

            @pl.when((c >= 0) & (c < chunks))
            def _():
                stage(side, c)

        @pl.when((tick == 0) & above)
        def _():
            do_copy(0).wait_recv()
            stat_copy(0).wait_recv()

        @pl.when((tick == 0) & below)
        def _():
            do_copy(1).wait_recv()
            stat_copy(1).wait_recv()

        @pl.when(tick < parts)
        def _():
            @pl.loop(0, group)
            def _(h):
                reverse(tick * group + h)

        @pl.when(tick == 0)
        def _():
            send_own(parts)

        @pl.when(tick < chunks)
        def _():
            input_share(tick)

        @pl.when(tick == chunks - 1)
        def _():
            for step in range(1, n_head):
                h_copy(step).start()


    for step in range(1, n_head):
        h_copy(step).wait()
    total = gx_acc[pl.ds(pl.multiple_of(me_head * share, share), share)]
    for step in range(1, n_head):
        total = total + gx_recv[step - 1]
    gx_ref[...] = total.astype(gx_ref.dtype)

    @pl.loop(0, chunks)
    def _(c):
        kind, where = place(c)
        gw_ref[kind, :, where] = part[c, me_seq]
        for side in range(2):
            @pl.when(fed[side])
            def _():
                hop(side, c, me_seq).wait_recv()
                gw_ref[kind, :, where] += flow[side, c, me_seq].astype(jnp.float32)

            @pl.loop(0, n_seq)
            def _(t):
                @pl.when(onward(side, t))
                def _():
                    hop(side, c, t).wait_send()

        for step in direct:
            dp_copy(c, step).wait_send()
        if relay:
            relay_copy(c, 1, 2).wait_send()

    def settle(slot, side):
        lat_copy(side).wait_send()
        do_copy(side).wait_send()
        stat_copy(side).wait_send()
        for step in range(1, n_head):
            pass_copy(slot, step).wait_send()

    @pl.when(below)
    def _():
        settle(0, 0)

    @pl.when(above)
    def _():
        settle(2, 1)

    for step in range(1, n_dp):
        clip_copy(step).wait_send()


def layer(slab_tokens, w_three, q_gain, k_gain, neighbours, upstream):
    n_dp, n_seq, n_head = (lax.axis_size(axis) for axis in ("dp", "seq", "head"))
    slab = slab_tokens.shape[0]
    three, model_width, head_width = w_three.shape
    heads = head_width // HD
    group = 3 if heads % 3 == 0 else 1
    width = group * HD
    chunks = three * heads // group
    block = model_width // n_dp
    rows = block // n_seq
    share = slab // n_head
    stat_rows = -(-2 * heads // 8) * 8
    vmem = pl.BlockSpec(memory_space=pltpu.VMEM)
    anywhere = pl.BlockSpec(memory_space=pl.ANY)
    dma = pltpu.SemaphoreType.DMA
    bf16, f32 = jnp.bfloat16, jnp.float32
    return pl.pallas_call(
        functools.partial(layer_kernel, n_dp, n_seq, n_head),
        out_shape=(
            jax.ShapeDtypeStruct((slab, head_width), bf16),
            jax.ShapeDtypeStruct((three, rows, head_width), f32),
            jax.ShapeDtypeStruct((share, model_width), bf16),
        ),
        in_specs=[anywhere, anywhere, vmem, vmem, vmem, anywhere],
        out_specs=(vmem, vmem, vmem),
        scratch_shapes=[
            pltpu.VMEM((chunks, slab, width), bf16),
            pltpu.VMEM((block, n_dp * slab), bf16),
            pltpu.VMEM((chunks, n_dp - 1, slab, width), bf16),
            pltpu.VMEM((chunks, n_seq, rows, width), f32),
            pltpu.VMEM((2, chunks, n_seq, rows, width), bf16),
            pltpu.VMEM((slab, model_width), f32),
            pltpu.VMEM((n_head - 1, share, model_width), f32),
            pltpu.VMEM((3, slab, model_width), bf16),
            pltpu.VMEM((three, model_width, head_width), bf16),
            pltpu.VMEM((3, slab, head_width), bf16),
            pltpu.VMEM((slab, head_width), f32),
            pltpu.VMEM((slab, head_width), f32),
            pltpu.VMEM((3, slab, head_width), bf16),
            pltpu.VMEM((3, slab, head_width), bf16),
            pltpu.VMEM((3, slab, head_width), bf16),
            pltpu.VMEM((slab, 3 * slab), f32),
            pltpu.VMEM((slab, 3 * slab), f32),
            pltpu.VMEM((slab, 128), f32),
            pltpu.VMEM((3, stat_rows, slab), f32),
            pltpu.VMEM((n_dp - 1, slab, block), bf16),
            dma((2,)),
            dma((chunks,)),
            dma((2,)),
            dma((2,)),
            dma((2, n_head - 1)),
            dma((2, n_head - 1)),
            dma((2,)),
            dma((2,)),
            dma((2,)),
            dma((2,)),
            dma((n_dp - 1,)),
            dma((n_dp - 1,)),
            dma((chunks, n_dp - 1)),
            dma((chunks, n_dp - 1)),
            dma((2, chunks, n_seq)),
            dma((2, chunks, n_seq)),
            dma((n_head - 1,)),
            dma((n_head - 1,)),
        ],
        compiler_params=pltpu.CompilerParams(
            collective_id=0, has_side_effects=True, vmem_limit_bytes=60 * 1024 * 1024
        ),
        name="layer",
    )(slab_tokens, w_three, q_gain.reshape(1, HD), k_gain.reshape(1, HD), neighbours, upstream)


def local(latents, w_qkv, q_gain, k_gain, neighbours, grad_out):
    w_three = jnp.transpose(w_qkv, (1, 0, 2))
    attn_out, grad_w, grad_x = layer(
        latents[0], w_three, q_gain, k_gain, neighbours, grad_out[0]
    )
    return (attn_out[None], grad_x[None], jnp.transpose(grad_w, (1, 0, 2)))


def solution(mesh):
    in_specs = (P("dp", "seq", None), P(None, None, "head"), P(), P(), P(), P("dp", "seq", "head"))
    out_specs = (
        P("dp", "seq", "head"),
        P("dp", ("seq", "head"), None),
        P(("dp", "seq"), None, "head"),
    )
    return jax.shard_map(local, mesh=mesh, in_specs=in_specs, out_specs=out_specs, check_vma=False)
```
